128 devices in a mesh: gx: 16 (over z, y), gy: 8 (over x, core).
Axes of the slice: x: 4, y: 4, z: 4, core: 2. Of those that a mesh axis runs over, the one named last changes fastest.
Arguments:
- voxel_xyz: float32 [32768, 3, 128], P(('gx', 'gy')), may hold values from 0 to 1
- voxel_mass: float32 [32768, 128], P(('gx', 'gy')), may hold values from 1 to 64
- candidates: int32 [32768, 8], P(('gx', 'gy')), may hold values from 0 to 65535, as said below
- offload_plan: int32 [32768], P(('gx', 'gy')), may hold values from -1 to 16383, as said below
- seed_xyz: float32 [65536, 3, 128], P(('gx', 'gy')), may hold values from 0 to 1
- seed_pot: float32 [65536, 128], P(('gx', 'gy')), may hold values from -5 to 225
- seed_target: float32 [65536, 128], P(('gx', 'gy')), may hold values from 0.5 to 8
- seed_home: int32 [65536], replicated, may hold values from 0 to 65535, as said below
Outputs:
- dual_pot: float32 [16384, 128], P(('gx', 'gy'))
- seed_moments: float32 [65536, 4, 128], P(('gx', 'gy'))
- new_pot: float32 [65536, 128], P(('gx', 'gy'))
The draws below stay inside these ranges and needn't reach their ends.
Inputs may be any that keep to these rules, and one draw needn't show every extreme that they name: `candidates`: the 8 ids of one voxel block are distinct seed blocks whose stored rows lie on the block's own device or on the devices one step lower or higher along gx (wrapping), with the same gy index. `offload_plan`: -1 marks a slot with no voxels. Otherwise the value is the row of dual_pot that the block fills; that row lies on a device with the same gx index, and every row is filled by exactly one block. The occupied slots of one device go to the rows of any one device in groups of exactly 32 blocks or not at all. `seed_home`: A permutation of the stored rows.
All inputs are finite; a program needn't handle non-finite values.
Results may differ from the reference program's by a relative error of at most 0.0003.
Values sent between devices are 32-bit elements; how exact they have to be, the bound alone decides.
A program may use at most 64 MiB of HBM per device.

```python
import math
import jax
import jax.numpy as jnp
from jax import lax

BS = 128
KC = 8
PAIR_CAP = 32
ACTIVE_POTENTIAL = 128
VB_DEV = 256
SB_DEV = 512
VOX_BLOCKS = 32768
SEED_BLOCKS = 65536
VOX_ROWS = 16384
N_GX = 16
N_GY = 8
DEVICES = 128


def distinct_order(key, shape):
    length = shape[-1]
    affinity_table = jax.random.randint(key, shape, 0, 1 << 20) * length + jnp.arange(length, dtype=jnp.int32)
    return jnp.argsort(affinity_table, axis=-1).astype(jnp.int32)


def build_layout(key):
    base = jax.random.fold_in(key, 7)
    k_home, chosen_candidate_index, k_order, k_slot, k_row = jax.random.split(base, 5)
    seed_home = jax.random.permutation(k_home, SEED_BLOCKS).astype(jnp.int32)
    stored_id = jnp.zeros((SEED_BLOCKS,), jnp.int32).at[seed_home].set(jnp.arange(SEED_BLOCKS, dtype=jnp.int32))
    pool_size = 3 * SB_DEV
    ranks = jax.random.randint(chosen_candidate_index, (VOX_BLOCKS, pool_size), 0, 1 << 20) * pool_size + jnp.arange(pool_size, dtype=jnp.int32)[None, :]
    picked = lax.top_k(ranks, KC)[1].astype(jnp.int32)
    home_dev = jnp.arange(VOX_BLOCKS, dtype=jnp.int32) // VB_DEV
    home_x = home_dev // N_GY
    home_y = home_dev % N_GY
    offset = picked // SB_DEV - 1
    owner = (home_x[:, None] + offset + N_GX) % N_GX * N_GY + home_y[:, None]
    stored = owner * SB_DEV + picked % SB_DEV
    candidates = stored_id[stored]
    group_size = N_GY
    half_count = group_size // 2
    order = distinct_order(k_order, (N_GX, group_size))
    rank = jnp.argsort(order, axis=1).astype(jnp.int32)
    sender = jnp.arange(group_size, dtype=jnp.int32)[None, :, None, None]
    dest = jnp.arange(group_size, dtype=jnp.int32)[None, None, :, None]
    item = jnp.arange(PAIR_CAP, dtype=jnp.int32)[None, None, None, :]
    sender_rank = rank[:, :, None, None]
    valid = sender_rank < half_count
    group_start = jnp.arange(N_GX, dtype=jnp.int32)[:, None, None, None] * group_size
    sender_dev = group_start + sender
    receiving_processor = group_start + dest
    slot_perm = distinct_order(k_slot, (DEVICES, VB_DEV))
    row_perm = distinct_order(k_row, (DEVICES, ACTIVE_POTENTIAL))
    slot = slot_perm[sender_dev, dest * PAIR_CAP + item]
    row = row_perm[receiving_processor, jnp.minimum(sender_rank, half_count - 1) * PAIR_CAP + item] + receiving_processor * ACTIVE_POTENTIAL
    full_shape = (N_GX, group_size, group_size, PAIR_CAP)
    flat_slot = sender_dev * VB_DEV + slot
    where_slot = jnp.broadcast_to(jnp.where(valid, flat_slot, VOX_BLOCKS), full_shape)
    row = jnp.broadcast_to(row, full_shape)
    plan = jnp.full((VOX_BLOCKS,), -1, jnp.int32).at[where_slot.reshape(-1)].set(row.reshape(-1), mode='drop')
    return (candidates, plan, seed_home)


def draw_candidates(key, part):
    return build_layout(key)[0]


def draw_offload_plan(key, part):
    return build_layout(key)[1]


def draw_seed_home(key, part):
    return build_layout(key)[2]


def draw_seed_pot(key, part):
    k_base = jax.random.fold_in(key, 0)
    return jnp.clip(jax.random.normal(k_base, (SEED_BLOCKS, BS), jnp.float32), -5.0, 5.0)


def level_of(stream_key, dims, cuts, least, high):
    loudness, own = 1.0, jax.random.fold_in(stream_key, 6)
    for axis_at, shards_of in cuts:
        steps = jnp.exp(jax.random.uniform(jax.random.fold_in(own, axis_at), (shards_of,), jnp.float32, least / len(cuts), high / len(cuts)))
        loudness = loudness * jnp.repeat(steps, dims[axis_at] // shards_of).reshape([-1 if axis == axis_at else 1 for axis in range(len(dims))])
    return loudness


def setup_inputs(seed: int = 0) -> dict:
    keys = jax.random.split(jax.random.key(seed), 9)
    return {
        "voxel_xyz": jnp.clip(1.0 * jax.random.uniform(keys[0], (VOX_BLOCKS, 3, BS), jnp.float32) ** level_of(keys[0], (VOX_BLOCKS, 3, BS), ((0, 128),), -0.2, 0.2), 0.0, 1.0),
        "voxel_mass": jnp.clip(jnp.exp(math.log(64.0) - 4.158883 * jax.random.uniform(keys[1], (VOX_BLOCKS, BS), jnp.float32) ** level_of(keys[1], (VOX_BLOCKS, BS), ((0, 128),), -0.2, 0.2)), 1.0, 64.0),
        "candidates": draw_candidates(jax.random.fold_in(keys[8], 71), 0),
        "offload_plan": draw_offload_plan(jax.random.fold_in(keys[8], 71), 0),
        "seed_xyz": jnp.clip(1.0 * jax.random.uniform(keys[4], (SEED_BLOCKS, 3, BS), jnp.float32) ** level_of(keys[4], (SEED_BLOCKS, 3, BS), ((0, 128),), -0.2, 0.2), 0.0, 1.0),
        "seed_pot": draw_seed_pot(jax.random.fold_in(keys[8], 71), 0),
        "seed_target": jnp.clip(jnp.exp(math.log(8.0) - 2.7725887 * jax.random.uniform(keys[6], (SEED_BLOCKS, BS), jnp.float32) ** level_of(keys[6], (SEED_BLOCKS, BS), ((0, 128),), -0.2, 0.2)), 0.5, 8.0),
        "seed_home": draw_seed_home(jax.random.fold_in(keys[8], 71), 0),
    }


smoothing_parameter = 0.05
step_rate = 0.5


def block_group(positions, masses, seed_data):
    block_count = seed_data.shape[0]
    pick_count = seed_data.shape[1]
    lane_count = seed_data.shape[3]
    seed_coord = jnp.transpose(seed_data[:, :, :3, :], (0, 2, 1, 3)).reshape(block_count, 3, pick_count * lane_count)
    centroid_kantorovich_price = seed_data[:, :, 3, :].reshape(block_count, pick_count * lane_count)
    quadratic_separation = (positions[:, 0, :, None] - seed_coord[:, 0, None, :]) ** 2
    quadratic_separation = quadratic_separation + (positions[:, 1, :, None] - seed_coord[:, 1, None, :]) ** 2
    quadratic_separation = quadratic_separation + (positions[:, 2, :, None] - seed_coord[:, 2, None, :]) ** 2
    affinity_table = centroid_kantorovich_price[:, None, :] - quadratic_separation / smoothing_parameter
    peak_score = jnp.max(affinity_table, axis=2, keepdims=True)
    unnormalized_affinity = jnp.exp(affinity_table - peak_score)
    denominator = jnp.sum(unnormalized_affinity, axis=2, keepdims=True)
    transport = masses[:, :, None] * (unnormalized_affinity / denominator)
    factors = jnp.concatenate([jnp.ones_like(positions[:, :1, :]), positions], axis=1)
    moment = jnp.einsum("nci,nij->ncj", factors, transport, precision=lax.Precision.HIGHEST)
    moment = jnp.transpose(moment.reshape(block_count, 4, pick_count, lane_count), (0, 2, 1, 3))
    dual_value = -(peak_score[:, :, 0] + jnp.log(denominator[:, :, 0]))
    return moment, dual_value


def reference(voxel_xyz, voxel_mass, candidates, offload_plan, seed_xyz, seed_pot, seed_target, seed_home):
    rows_all = VOX_ROWS
    slot_total = offload_plan.shape[0]
    target_rows = jnp.where(offload_plan < 0, rows_all, offload_plan).astype(jnp.int32)
    source = jnp.zeros((rows_all,), jnp.int32).at[target_rows].set(jnp.arange(slot_total, dtype=jnp.int32), mode="drop")
    seed_table = jnp.concatenate([seed_xyz, seed_pot[:, None, :]], axis=1)
    per_step = 8
    grouped = source.reshape(rows_all // per_step, per_step)

    def visit(seed_mass_sums, blocks):
        stored = seed_home[candidates[blocks]].astype(jnp.int32)
        moment, dual_value = block_group(voxel_xyz[blocks], voxel_mass[blocks], seed_table[stored])
        seed_mass_sums = seed_mass_sums.at[stored.reshape(-1)].add(moment.reshape(-1, 4, BS))
        return seed_mass_sums, dual_value

    start_sums = jnp.zeros((SEED_BLOCKS, 4, BS), jnp.float32)
    seed_mass_sums, dual_parts = lax.scan(visit, start_sums, grouped)
    dual_pot = dual_parts.reshape(rows_all, BS)
    new_pot = seed_pot + step_rate * (seed_target - seed_mass_sums[:, 0, :])
    return dual_pot, seed_mass_sums, new_pot
```

```python
import math

import jax
import jax.numpy as jnp
from jax import lax
from jax.experimental import pallas as pl
from jax.experimental.pallas import tpu as pltpu
from jax.sharding import PartitionSpec as P

BS = 128
KC = 8
PAIR_CAP = 32
VB = 256
SB = 512
POOL = 3 * SB
N_GX = 16
N_GY = 8
ROWS = 128

EPS = 0.05
STEP = 0.5
LOG2E = math.log2(math.e)
LN2 = math.log(2.0)


def prep_kernel(cand, plan, home, pidx, order, pos, send_row, count):
    me = lax.axis_index("gx")

    @pl.loop(0, VB)
    def _(i):
        send_row[i] = -1

    def slot(v, carry):
        n, ranks = carry
        p = plan[v]

        def occupied(n, *ranks):
            dest = (p // ROWS) % N_GY
            rank = ranks[0]
            for g in range(1, N_GY):
                rank = jnp.where(dest == g, ranks[g], rank)
            order[n] = v
            at = dest * PAIR_CAP + rank
            pos[n] = at
            send_row[at] = p % ROWS
            for k in range(KC):
                s = home[cand[v * KC + k]]
                near = (s // (SB * N_GY) - me + 1 + N_GX) % N_GX
                pidx[n * KC + k] = near * SB + s % SB
            return (n + 1,) + tuple(
                jnp.where(dest == g, ranks[g] + 1, ranks[g]) for g in range(N_GY)
            )

        out = lax.cond(p >= 0, occupied, lambda n, *r: (n,) + tuple(r), n, *ranks)
        return out[0], tuple(out[1:])

    zero = jnp.int32(0)
    n, _ = lax.fori_loop(0, VB, slot, (zero, (zero,) * N_GY))
    count[0] = n


def prep(cand, plan, home):
    smem = pl.BlockSpec(memory_space=pltpu.SMEM)
    i32 = lambda n: jax.ShapeDtypeStruct((n,), jnp.int32)
    return pl.pallas_call(
        prep_kernel,
        in_specs=[smem] * 3,
        out_specs=[smem] * 5,
        out_shape=[i32(VB * KC), i32(VB), i32(VB), i32(VB), i32(1)],
        name="prep",
    )(cand, plan, home)


def bf(x):
    return x.astype(jnp.bfloat16)


def f32(x):
    return x.astype(jnp.float32)


def work_kernel(pidx, order, pos, count, vox, mass, table, mom, dual, ypool, split, wrow):
    n = count[0]
    sub = lax.broadcasted_iota(jnp.int32, (8, BS), 0)
    low = sub < 4
    mom[...] = jnp.zeros_like(mom)
    dual[...] = jnp.zeros_like(dual)

    @pl.loop(0, POOL // 8)
    def _(g):
        for j in range(8):
            t = table[g * 8 + j]
            a = jnp.concatenate([t, t], axis=0)
            hi = f32(bf(a))
            mid = f32(bf(a - hi))
            first = jnp.where(low, hi, mid)
            second = jnp.where(sub == 3, a - hi - mid, jnp.where(sub == 7, 1.0, first))
            ypool[g * 8 + j] = bf(jnp.concatenate([first, second], axis=0))

    def scores(t, slot):
        s = order[t]
        x = vox[s] - 0.5
        xh = f32(bf(x))
        xl = x - xh
        idx = [pidx[t * KC + k] for k in range(KC)]
        top = table[idx[0], 3:4, :]
        for k in range(1, KC):
            top = jnp.maximum(top, table[idx[k], 3:4, :])
        top = f32(bf(jnp.max(top, axis=1, keepdims=True)))
        top = jnp.broadcast_to(top, (1, BS))
        one = jnp.ones((1, BS), jnp.float32)
        xa = bf(jnp.concatenate([xh, one, xh, one, xl, one, xl, -top], axis=0))
        part = None
        for c in range(KC // 2):
            y = jnp.concatenate([ypool[idx[2 * c]], ypool[idx[2 * c + 1]]], axis=1)
            sc = lax.dot_general(
                xa, y, (((0,), (0,)), ((), ())), preferred_element_type=jnp.float32
            )
            e = jnp.exp2(sc)
            eh = bf(e)
            split[slot, 0:BS, c * 256 : (c + 1) * 256] = eh
            split[slot, BS : 2 * BS, c * 256 : (c + 1) * 256] = bf(e - f32(eh))
            p = e[:, :BS] + e[:, BS:]
            part = p if part is None else part + p
        d = jnp.sum(part.T, axis=0, keepdims=True)
        sq = jnp.sum(x * x, axis=0, keepdims=True)
        dual[pl.ds(pos[t], 1), :] = (1.0 / EPS) * sq - LN2 * (top + jnp.log2(d))
        wrow[pl.ds(slot, 1), :] = mass[pl.ds(s, 1), :] / d

    def moments(t, slot):
        s = order[t]
        w = wrow[pl.ds(slot, 1), :]
        f = jnp.concatenate([w, vox[s] * w], axis=0)
        fh = f32(bf(f))
        f8 = bf(jnp.concatenate([fh, f - fh], axis=0))
        m = jnp.dot(
            jnp.concatenate([f8, f8], axis=1), split[slot], preferred_element_type=jnp.float32
        )
        for k in range(KC):
            i = pidx[t * KC + k]
            mom[i] += m[:, k * BS : (k + 1) * BS]

    @pl.when(n > 0)
    def _():
        scores(0, 0)

        @pl.loop(0, n // 2)
        def _(h):
            t = 2 * h + 1
            moments(t - 1, 0)
            scores(t, 1)
            moments(t, 1)
            scores(jnp.minimum(t + 1, n - 1), 0)


def work(pidx, order, pos, count, vox, mass, table):
    vm = pl.BlockSpec(memory_space=pltpu.VMEM)
    smem = pl.BlockSpec(memory_space=pltpu.SMEM)
    return pl.pallas_call(
        work_kernel,
        in_specs=[smem] * 4 + [vm] * 3,
        out_specs=[vm, vm],
        out_shape=[
            jax.ShapeDtypeStruct((POOL, 8, BS), jnp.float32),
            jax.ShapeDtypeStruct((VB, BS), jnp.float32),
        ],
        scratch_shapes=[
            pltpu.VMEM((POOL, 16, BS), jnp.bfloat16),
            pltpu.VMEM((2, 2 * BS, KC * BS), jnp.bfloat16),
            pltpu.VMEM((8, BS), jnp.float32),
        ],
        compiler_params=pltpu.CompilerParams(vmem_limit_bytes=56 << 20),
        name="work",
    )(pidx, order, pos, count, vox, mass, table)


def shifted(value, steps):
    pairs = [(source, (source + steps) % N_GX) for source in range(N_GX)]
    return lax.ppermute(value, "gx", pairs)


def on_device(
    voxel_xyz, voxel_mass, candidates, offload_plan, seed_xyz, seed_pot, seed_target, seed_home
):
    y = seed_xyz - 0.5
    offset = LOG2E * (seed_pot - (1.0 / EPS) * jnp.sum(y * y, axis=1))
    table = jnp.concatenate([(2.0 * LOG2E / EPS) * y, offset[:, None, :]], axis=1)
    pool = jnp.concatenate([shifted(table, 1), table, shifted(table, -1)], axis=0)
    pidx, order, pos, send_row, count = prep(candidates.reshape(-1), offload_plan, seed_home)
    mom, dual = work(pidx, order, pos, count, voxel_xyz, voxel_mass, pool)
    sums = mom[:, :4] + mom[:, 4:]
    index = send_row.astype(jnp.float32).reshape(N_GY, PAIR_CAP)
    index = jnp.pad(index, ((0, 0), (0, BS - PAIR_CAP)))[:, None, :]
    send = jnp.concatenate([dual.reshape(N_GY, PAIR_CAP, BS), index], axis=1)
    got = lax.all_to_all(send, "gy", split_axis=0, concat_axis=0, tiled=True)
    fill = got[:, PAIR_CAP, :PAIR_CAP].reshape(1, -1)
    hot = (lax.broadcasted_iota(jnp.int32, (ROWS, 1), 0).astype(jnp.float32) == fill).astype(
        jnp.float32
    )
    dual_pot = jnp.dot(
        hot, got[:, :PAIR_CAP].reshape(-1, BS), precision=lax.Precision.HIGHEST
    )
    seed_moments = (
        sums[SB : 2 * SB] + shifted(sums[:SB], -1) + shifted(sums[2 * SB :], 1)
    )
    new_pot = seed_pot + STEP * (seed_target - seed_moments[:, 0, :])
    return (dual_pot, seed_moments, new_pot)


def solution(mesh):
    return jax.shard_map(
        on_device,
        mesh=mesh,
        in_specs=(
            P(("gx", "gy"), None, None),
            P(("gx", "gy"), None),
            P(("gx", "gy"), None),
            P(("gx", "gy")),
            P(("gx", "gy"), None, None),
            P(("gx", "gy"), None),
            P(("gx", "gy"), None),
            P(),
        ),
        out_specs=(P(("gx", "gy"), None), P(("gx", "gy"), None, None), P(("gx", "gy"), None)),
        check_vma=False,
    )
```

```python
import math

import jax
import jax.numpy as jnp
from jax import lax
from jax.experimental import pallas as pl
from jax.experimental.pallas import tpu as pltpu
from jax.sharding import PartitionSpec as P

BS = 128
KC = 8
PAIR_CAP = 32
VB = 256
SB = 512
POOL = 3 * SB
N_GX = 16
N_GY = 8
ROWS = 128
SLOTS = 4

EPS = 0.05
STEP = 0.5
LOG2E = math.log2(math.e)
LN2 = math.log(2.0)

VMEM = pl.BlockSpec(memory_space=pltpu.VMEM)
SMEM = pl.BlockSpec(memory_space=pltpu.SMEM)


def bf(x):
    return x.astype(jnp.bfloat16)


def f32(x):
    return x.astype(jnp.float32)


def prep_kernel(cand, plan, home, pidx, order, pos, send_row, count, ranks):
    me = lax.axis_index("gx")
    for g in range(N_GY):
        ranks[g] = 0

    @pl.loop(0, VB // 16)
    def _(i):
        for j in range(16):
            send_row[i * 16 + j] = -1

    def slots(h, n):
        for u in range(2):
            v = 2 * h + u
            p = plan[v]
            occupied = (p >= 0).astype(jnp.int32)
            for k in range(KC):
                s = home[cand[k, v]]
                near = ((s >> 12) - me + 1) & 15
                pidx[n * KC + k] = (near << 9) | (s & 511)
            dest = (p >> 7) & 7
            rank = ranks[dest]
            ranks[dest] = rank + occupied
            at = jnp.where(p >= 0, dest * PAIR_CAP + rank, VB)
            order[n] = v
            pos[n] = at
            send_row[at] = p & 127
            n = n + occupied
        return n

    count[0] = lax.fori_loop(0, VB // 2, slots, jnp.int32(0))


def prep(cand, plan, home):
    i32 = lambda n: jax.ShapeDtypeStruct((n,), jnp.int32)
    return pl.pallas_call(
        prep_kernel,
        in_specs=[SMEM] * 3,
        out_specs=[SMEM] * 5,
        out_shape=[i32(VB * KC + KC), i32(VB + 8), i32(VB + 8), i32(VB + 8), i32(1)],
        scratch_shapes=[pltpu.SMEM((N_GY,), jnp.int32)],
        cost_estimate=pl.CostEstimate(flops=1000000, bytes_accessed=30000000, transcendentals=0),
        name="prep",
    )(cand, plan, home)


BUFFERS = ("split", "xat", "part", "top", "f8")


def work_kernel(
    pidx, order, pos, count, vox, mass, low_in, own_in, high_in,
    low_out, own_out, high_out, dual, mom, ypool, *scratch,
):
    n = count[0]
    size = len(BUFFERS)
    bufs = [dict(zip(BUFFERS, scratch[i * size : (i + 1) * size])) for i in range(SLOTS)]
    sub = lax.broadcasted_iota(jnp.int32, (8, BS), 0)
    low = sub < 4
    dual[...] = jnp.zeros_like(dual)
    for q, table in enumerate((low_in, own_in, high_in)):

        @pl.loop(0, SB // 16)
        def _(g):
            for j in range(16):
                i = g * 16 + j
                t = table[pl.ds(i, 4, stride=SB), :]
                a = jnp.concatenate([t, t], axis=0)
                hi = f32(bf(a))
                mid = f32(bf(a - hi))
                first = jnp.where(low, hi, mid)
                second = jnp.where(sub == 3, a - hi - mid, jnp.where(sub == 7, 1.0, first))
                ypool[q * SB + i] = bf(jnp.concatenate([first, second], axis=0))
                mom[q * SB + i] = jnp.zeros((8, BS), jnp.float32)

    def prepare(t, b):
        s = order[t]
        x = vox[pl.ds(s, 3, stride=VB), :] - 0.5
        xh = f32(bf(x))
        xl = x - xh
        tops = [f32(ypool[pidx[t * KC + k], 0:8, :]) for k in range(KC)]
        while len(tops) > 1:
            tops = [jnp.maximum(a, c) for a, c in zip(tops[::2], tops[1::2])]
        top = jnp.max(tops[0][3:4], axis=1, keepdims=True)
        top = jnp.broadcast_to(top, (1, BS))
        one = jnp.ones((1, BS), jnp.float32)
        xa = jnp.concatenate([xh, one, xh, one, xl, one, xl, -top], axis=0)
        b["xat"][...] = bf(xa.T)
        b["top"][0:1, :] = top

    def weigh(t, b):
        idx = [pidx[t * KC + k] for k in range(KC)]
        xat = b["xat"][...]
        part = None
        for c in range(KC // 2):
            y = jnp.concatenate([ypool[idx[2 * c]], ypool[idx[2 * c + 1]]], axis=1)
            e = jnp.exp2(jnp.dot(xat, y, preferred_element_type=jnp.float32))
            eh = bf(e)
            b["split"][0:BS, c * 256 : (c + 1) * 256] = eh
            b["split"][BS : 2 * BS, c * 256 : (c + 1) * 256] = bf(e - f32(eh))
            p = e[:, :BS] + e[:, BS:]
            part = p if part is None else part + p
        b["part"][...] = part

    def norm(t, b):
        s = order[t]
        d = jnp.sum(b["part"][...].T, axis=0, keepdims=True)
        xr = vox[pl.ds(s, 3, stride=VB), :]
        x = xr - 0.5
        sq = jnp.sum(x * x, axis=0, keepdims=True)
        dual[pl.ds(pos[t], 1), :] = (1.0 / EPS) * sq - LN2 * (b["top"][0:1, :] + jnp.log2(d))
        w = mass[pl.ds(s, 1), :] / d
        f = jnp.concatenate([w, xr * w], axis=0)
        fh = f32(bf(f))
        f8 = bf(jnp.concatenate([fh, f - fh], axis=0))
        b["f8"][...] = jnp.concatenate([f8, f8], axis=1)

    def spread(t, b):
        m = jnp.dot(b["f8"][...], b["split"][...], preferred_element_type=jnp.float32)
        for k in range(KC):
            i = pidx[t * KC + k]
            mom[i] += m[:, k * BS : (k + 1) * BS]

    stages = (prepare, weigh, norm, spread)

    def step(t, slot, valid):
        for lag, stage in enumerate(stages):
            if valid(lag):
                stage(t - lag, bufs[(slot - lag) % SLOTS])

    @pl.when(n > 0)
    def _():
        for t in range(SLOTS):
            step(t, t, lambda lag: lag <= t)

        @pl.loop(0, (n - SLOTS) // SLOTS)
        def _(h):
            for u in range(SLOTS):
                step(SLOTS + SLOTS * h + u, u, lambda lag: True)

        for e in range(len(stages) - 1):
            step(n + e, e, lambda lag: lag > e)

    for q, out in enumerate((low_out, own_out, high_out)):

        @pl.loop(0, SB // 16)
        def _(g):
            for j in range(16):
                m = mom[q * SB + g * 16 + j]
                out[g * 16 + j] = m[0:4] + m[4:8]


def work(pidx, order, pos, count, vox, mass, low, own, high):
    moments = jax.ShapeDtypeStruct((SB, 4, BS), jnp.float32)
    scratch = [
        pltpu.VMEM((POOL, 8, BS), jnp.float32),
        pltpu.VMEM((POOL, 16, BS), jnp.bfloat16),
    ]
    scratch += [
        pltpu.VMEM((2 * BS, KC * BS), jnp.bfloat16),
        pltpu.VMEM((BS, 16), jnp.bfloat16),
        pltpu.VMEM((BS, BS), jnp.float32),
        pltpu.VMEM((8, BS), jnp.float32),
        pltpu.VMEM((8, 2 * BS), jnp.bfloat16),
    ] * SLOTS
    return pl.pallas_call(
        work_kernel,
        in_specs=[SMEM] * 4 + [VMEM] * 5,
        out_specs=[VMEM] * 4,
        out_shape=[moments] * 3 + [jax.ShapeDtypeStruct((VB, BS), jnp.float32)],
        scratch_shapes=scratch,
        compiler_params=pltpu.CompilerParams(vmem_limit_bytes=56 << 20),
        name="work",
    )(pidx, order, pos, count, vox, mass, low, own, high)


def shifted(value, steps):
    pairs = [(source, (source + steps) % N_GX) for source in range(N_GX)]
    return lax.ppermute(value, "gx", pairs)


def on_device(
    voxel_xyz, voxel_mass, candidates, offload_plan, seed_xyz, seed_pot, seed_target, seed_home
):
    y = jnp.transpose(seed_xyz, (1, 0, 2)) - 0.5
    offset = LOG2E * (seed_pot - (1.0 / EPS) * (y[0] * y[0] + y[1] * y[1] + y[2] * y[2]))
    table = jnp.concatenate([(2.0 * LOG2E / EPS) * y, offset[None]], axis=0)
    table = table.reshape(4 * SB, BS)
    vox = jnp.transpose(voxel_xyz, (1, 0, 2)).reshape(3 * VB, BS)
    pidx, order, pos, send_row, count = prep(candidates.T, offload_plan, seed_home)
    low, own, high, dual = work(
        pidx, order, pos, count, vox, voxel_mass, shifted(table, 1), table, shifted(table, -1)
    )
    index = send_row[:VB].astype(jnp.float32).reshape(N_GY, PAIR_CAP)
    index = jnp.pad(index, ((0, 0), (0, BS - PAIR_CAP)))[:, None, :]
    send = jnp.concatenate([dual.reshape(N_GY, PAIR_CAP, BS), index], axis=1)
    got = lax.all_to_all(send, "gy", split_axis=0, concat_axis=0, tiled=True)
    fill = got[:, PAIR_CAP, :PAIR_CAP].reshape(1, -1)
    hot = (lax.broadcasted_iota(jnp.int32, (ROWS, 1), 0).astype(jnp.float32) == fill).astype(
        jnp.float32
    )
    dual_pot = jnp.dot(
        hot, got[:, :PAIR_CAP].reshape(-1, BS), precision=lax.Precision.HIGHEST
    )
    seed_moments = own + shifted(low, -1) + shifted(high, 1)
    new_pot = seed_pot + STEP * (seed_target - seed_moments[:, 0, :])
    return (dual_pot, seed_moments, new_pot)


def solution(mesh):
    return jax.shard_map(
        on_device,
        mesh=mesh,
        in_specs=(
            P(("gx", "gy"), None, None),
            P(("gx", "gy"), None),
            P(("gx", "gy"), None),
            P(("gx", "gy")),
            P(("gx", "gy"), None, None),
            P(("gx", "gy"), None),
            P(("gx", "gy"), None),
            P(),
        ),
        out_specs=(P(("gx", "gy"), None), P(("gx", "gy"), None, None), P(("gx", "gy"), None)),
        check_vma=False,
    )
```

```python
import math

import jax
import jax.numpy as jnp
from jax import lax
from jax.experimental import pallas as pl
from jax.experimental.pallas import tpu as pltpu
from jax.sharding import PartitionSpec as P

BS = 128
KC = 8
PAIR_CAP = 32
VB = 256
SB = 512
POOL = 3 * SB
N_GX = 16
N_GY = 8
ROWS = 128
SLOTS = 4
TOGETHER = 2

EPS = 0.05
STEP = 0.5
LOG2E = math.log2(math.e)
LN2 = math.log(2.0)

VMEM = pl.BlockSpec(memory_space=pltpu.VMEM)
SMEM = pl.BlockSpec(memory_space=pltpu.SMEM)


def bf(x):
    return x.astype(jnp.bfloat16)


def f32(x):
    return x.astype(jnp.float32)


def prep_kernel(cand, plan, home, pidx, order, pos, send_row, count, ranks):
    me = lax.axis_index("gx")
    for g in range(N_GY):
        ranks[g] = 0

    @pl.loop(0, VB // 16)
    def _(i):
        for j in range(16):
            send_row[i * 16 + j] = -1

    def slots(h, n):
        for u in range(2):
            v = 2 * h + u
            p = plan[v]
            occupied = (p >= 0).astype(jnp.int32)
            for k in range(KC):
                s = home[cand[k, v]]
                near = ((s >> 12) - me + 1) & 15
                pidx[n * KC + k] = (near << 9) | (s & 511)
            dest = (p >> 7) & 7
            rank = ranks[dest]
            ranks[dest] = rank + occupied
            at = jnp.where(p >= 0, dest * PAIR_CAP + rank, VB)
            order[n] = v
            pos[n] = at
            send_row[at] = p & 127
            n = n + occupied
        return n

    count[0] = lax.fori_loop(0, VB // 2, slots, jnp.int32(0))


def prep(cand, plan, home):
    i32 = lambda n: jax.ShapeDtypeStruct((n,), jnp.int32)
    return pl.pallas_call(
        prep_kernel,
        in_specs=[SMEM] * 3,
        out_specs=[SMEM] * 5,
        out_shape=[i32(VB * KC + KC), i32(VB + 8), i32(VB + 8), i32(VB + 8), i32(1)],
        scratch_shapes=[pltpu.SMEM((N_GY,), jnp.int32)],
        cost_estimate=pl.CostEstimate(flops=1000000, bytes_accessed=30000000, transcendentals=0),
        name="prep",
    )(cand, plan, home)


BUFFERS = ("split", "xat", "part", "top", "f8")


def work_kernel(
    pidx, order, pos, count, vox, mass, low_in, own_in, high_in,
    low_out, own_out, high_out, dual, mom, ypool, *scratch,
):
    n = count[0]
    size = len(BUFFERS)
    bufs = [dict(zip(BUFFERS, scratch[i * size : (i + 1) * size])) for i in range(SLOTS * TOGETHER)]
    sub = lax.broadcasted_iota(jnp.int32, (8, BS), 0)
    low = sub < 4
    dual[...] = jnp.zeros_like(dual)
    for q, table in enumerate((low_in, own_in, high_in)):

        @pl.loop(0, SB // 16)
        def _(g):
            for j in range(16):
                i = g * 16 + j
                t = table[pl.ds(i, 4, stride=SB), :]
                a = jnp.concatenate([t, t], axis=0)
                hi = f32(bf(a))
                mid = f32(bf(a - hi))
                first = jnp.where(low, hi, mid)
                second = jnp.where(sub == 3, a - hi - mid, jnp.where(sub == 7, 1.0, first))
                ypool[q * SB + i] = bf(jnp.concatenate([first, second], axis=0))
                mom[q * SB + i] = jnp.zeros((8, BS), jnp.float32)

    def prepare(t, b):
        s = order[t]
        x = vox[pl.ds(s, 3, stride=VB), :] - 0.5
        xh = f32(bf(x))
        xl = x - xh
        tops = [f32(ypool[pidx[t * KC + k], 0:8, :]) for k in range(KC)]
        while len(tops) > 1:
            tops = [jnp.maximum(a, c) for a, c in zip(tops[::2], tops[1::2])]
        top = jnp.max(tops[0][3:4], axis=1, keepdims=True)
        top = jnp.broadcast_to(top, (1, BS))
        one = jnp.ones((1, BS), jnp.float32)
        xa = jnp.concatenate([xh, one, xh, one, xl, one, xl, -top], axis=0)
        b["xat"][...] = bf(xa.T)
        b["top"][0:1, :] = top

    def weigh_and_spread(t, b, told, bold):
        part = None
        for c in range(KC // 2):
            if t is not None:
                y = [ypool[pidx[t * KC + 2 * c + j]] for j in range(2)]
                sc = jnp.dot(
                    b["xat"][...],
                    jnp.concatenate(y, axis=1),
                    preferred_element_type=jnp.float32,
                )
            if told is not None:
                e2 = jnp.concatenate([bold["split"][2 * c], bold["split"][2 * c + 1]], axis=1)
                m = jnp.dot(bold["f8"][...], e2, preferred_element_type=jnp.float32)
                for j in range(2):
                    mom[pidx[told * KC + 2 * c + j]] += m[:, j * BS : (j + 1) * BS]
            if t is not None:
                e = jnp.exp2(sc)
                eh = bf(e)
                el = bf(e - f32(eh))
                for j in range(2):
                    b["split"][2 * c + j, 0:BS, :] = eh[:, j * BS : (j + 1) * BS]
                    b["split"][2 * c + j, BS:, :] = el[:, j * BS : (j + 1) * BS]
                p = e[:, :BS] + e[:, BS:]
                part = p if part is None else part + p
        if t is not None:
            b["part"][...] = part

    def norm(t, b):
        s = order[t]
        d = jnp.sum(b["part"][...].T, axis=0, keepdims=True)
        xr = vox[pl.ds(s, 3, stride=VB), :]
        x = xr - 0.5
        sq = jnp.sum(x * x, axis=0, keepdims=True)
        dual[pl.ds(pos[t], 1), :] = (1.0 / EPS) * sq - LN2 * (b["top"][0:1, :] + jnp.log2(d))
        w = mass[pl.ds(s, 1), :] / d
        f = jnp.concatenate([w, xr * w], axis=0)
        fh = f32(bf(f))
        f8 = bf(jnp.concatenate([fh, f - fh], axis=0))
        b["f8"][...] = jnp.concatenate([f8, f8], axis=1)

    def step(g, slot, valid):
        for stage in range(3):
            for u in range(TOGETHER):
                at = lambda lag: (g - lag) * TOGETHER + u if valid(lag) else None
                buf = lambda lag: bufs[((slot - lag) % SLOTS) * TOGETHER + u]
                if stage == 0 and valid(0):
                    prepare(at(0), buf(0))
                if stage == 1 and (valid(1) or valid(3)):
                    weigh_and_spread(at(1), buf(1), at(3), buf(3))
                if stage == 2 and valid(2):
                    norm(at(2), buf(2))

    groups = n // TOGETHER

    @pl.when(n > 0)
    def _():
        for g in range(SLOTS):
            step(g, g, lambda lag: lag <= g)

        @pl.loop(0, (groups - SLOTS) // SLOTS)
        def _(h):
            for u in range(SLOTS):
                step(SLOTS + SLOTS * h + u, u, lambda lag: True)

        for e in range(3):
            step(groups + e, e, lambda lag: lag > e)

    for q, out in enumerate((low_out, own_out, high_out)):

        @pl.loop(0, SB // 16)
        def _(g):
            for j in range(16):
                m = mom[q * SB + g * 16 + j]
                out[g * 16 + j] = m[0:4] + m[4:8]


def work(pidx, order, pos, count, vox, mass, low, own, high):
    moments = jax.ShapeDtypeStruct((SB, 4, BS), jnp.float32)
    scratch = [
        pltpu.VMEM((POOL, 8, BS), jnp.float32),
        pltpu.VMEM((POOL, 16, BS), jnp.bfloat16),
    ]
    scratch += [
        pltpu.VMEM((KC, 2 * BS, BS), jnp.bfloat16),
        pltpu.VMEM((BS, 16), jnp.bfloat16),
        pltpu.VMEM((BS, BS), jnp.float32),
        pltpu.VMEM((8, BS), jnp.float32),
        pltpu.VMEM((8, 2 * BS), jnp.bfloat16),
    ] * (SLOTS * TOGETHER)
    return pl.pallas_call(
        work_kernel,
        in_specs=[SMEM] * 4 + [VMEM] * 5,
        out_specs=[VMEM] * 4,
        out_shape=[moments] * 3 + [jax.ShapeDtypeStruct((VB, BS), jnp.float32)],
        scratch_shapes=scratch,
        compiler_params=pltpu.CompilerParams(vmem_limit_bytes=56 << 20),
        name="work",
    )(pidx, order, pos, count, vox, mass, low, own, high)


def shifted(value, steps):
    pairs = [(source, (source + steps) % N_GX) for source in range(N_GX)]
    return lax.ppermute(value, "gx", pairs)


def on_device(
    voxel_xyz, voxel_mass, candidates, offload_plan, seed_xyz, seed_pot, seed_target, seed_home
):
    y = jnp.transpose(seed_xyz, (1, 0, 2)) - 0.5
    offset = LOG2E * (seed_pot - (1.0 / EPS) * (y[0] * y[0] + y[1] * y[1] + y[2] * y[2]))
    table = jnp.concatenate([(2.0 * LOG2E / EPS) * y, offset[None]], axis=0)
    table = table.reshape(4 * SB, BS)
    vox = jnp.transpose(voxel_xyz, (1, 0, 2)).reshape(3 * VB, BS)
    pidx, order, pos, send_row, count = prep(candidates.T, offload_plan, seed_home)
    low, own, high, dual = work(
        pidx, order, pos, count, vox, voxel_mass, shifted(table, 1), table, shifted(table, -1)
    )
    index = send_row[:VB].astype(jnp.float32).reshape(N_GY, PAIR_CAP)
    index = jnp.pad(index, ((0, 0), (0, BS - PAIR_CAP)))[:, None, :]
    send = jnp.concatenate([dual.reshape(N_GY, PAIR_CAP, BS), index], axis=1)
    got = lax.all_to_all(send, "gy", split_axis=0, concat_axis=0, tiled=True)
    fill = got[:, PAIR_CAP, :PAIR_CAP].reshape(1, -1)
    hot = (lax.broadcasted_iota(jnp.int32, (ROWS, 1), 0).astype(jnp.float32) == fill).astype(
        jnp.float32
    )
    dual_pot = jnp.dot(
        hot, got[:, :PAIR_CAP].reshape(-1, BS), precision=lax.Precision.HIGHEST
    )
    seed_moments = own + shifted(low, -1) + shifted(high, 1)
    new_pot = seed_pot + STEP * (seed_target - seed_moments[:, 0, :])
    return (dual_pot, seed_moments, new_pot)


def solution(mesh):
    return jax.shard_map(
        on_device,
        mesh=mesh,
        in_specs=(
            P(("gx", "gy"), None, None),
            P(("gx", "gy"), None),
            P(("gx", "gy"), None),
            P(("gx", "gy")),
            P(("gx", "gy"), None, None),
            P(("gx", "gy"), None),
            P(("gx", "gy"), None),
            P(),
        ),
        out_specs=(P(("gx", "gy"), None), P(("gx", "gy"), None, None), P(("gx", "gy"), None)),
        check_vma=False,
    )
```

```python
import math

import jax
import jax.numpy as jnp
from jax import lax
from jax.experimental import pallas as pl
from jax.experimental.pallas import tpu as pltpu
from jax.sharding import PartitionSpec as P

BS = 128
KC = 8
PAIR_CAP = 32
VB = 256
SB = 512
POOL = 3 * SB
N_GX = 16
N_GY = 8
ROWS = 128
GROUP = 40
SLOTS = 4
TOGETHER = 2

EPS = 0.05
STEP = 0.5
LOG2E = math.log2(math.e)
LN2 = math.log(2.0)

VMEM = pl.BlockSpec(memory_space=pltpu.VMEM)
SMEM = pl.BlockSpec(memory_space=pltpu.SMEM)
ANY = pl.BlockSpec(memory_space=pl.ANY)
MESH = pl.DeviceIdType.MESH


def bf(x):
    return x.astype(jnp.bfloat16)


def f32(x):
    return x.astype(jnp.float32)


def meet(peers):
    barrier = pltpu.get_barrier_semaphore()
    for peer in peers:
        pl.semaphore_signal(barrier, inc=1, device_id=peer, device_id_type=MESH)
    pl.semaphore_wait(barrier, len(peers))


def exchange_kernel(
    xyz, pot, cand, home_hbm, own, low, high, pidx, home, home_sem, send_sem, recv_sem
):
    x, g = lax.axis_index("gx"), lax.axis_index("gy")
    below, above = (x + N_GX - 1) % N_GX, (x + 1) % N_GX
    fetch = pltpu.make_async_copy(home_hbm, home, home_sem)
    fetch.start()

    @pl.loop(0, SB // 64)
    def _(i):
        at = pl.multiple_of(i * 64, 64)
        square = None
        for c in range(3):
            y = xyz[c, pl.ds(at, 64), :] - 0.5
            own[pl.ds(c * SB + at, 64), :] = (2.0 * LOG2E / EPS) * y
            square = y * y if square is None else square + y * y
        own[pl.ds(3 * SB + at, 64), :] = LOG2E * (pot[pl.ds(at, 64), :] - (1.0 / EPS) * square)

    meet([(below, g), (above, g)])
    up = pltpu.make_async_remote_copy(
        own, low, send_sem.at[0], recv_sem.at[0], device_id=(above, g), device_id_type=MESH
    )
    down = pltpu.make_async_remote_copy(
        own, high, send_sem.at[1], recv_sem.at[1], device_id=(below, g), device_id_type=MESH
    )
    up.start()
    down.start()
    fetch.wait()

    @pl.loop(0, VB // 2)
    def _(h):
        for u in range(2):
            v = 2 * h + u
            for k in range(KC):
                s = home[cand[k, v]]
                pidx[v * KC + k] = ((((s >> 12) - x + 1) & 15) << 9) | (s & 511)

    up.wait()
    down.wait()


def exchange(xyz, pot, cand, home):
    table = jax.ShapeDtypeStruct((4 * SB, BS), jnp.float32)
    return pl.pallas_call(
        exchange_kernel,
        in_specs=[VMEM, VMEM, SMEM, ANY],
        out_specs=[VMEM] * 3 + [SMEM],
        out_shape=[table] * 3 + [jax.ShapeDtypeStruct((VB * KC,), jnp.int32)],
        scratch_shapes=[
            pltpu.SMEM((N_GX * N_GY * SB,), jnp.int32),
            pltpu.SemaphoreType.DMA(()),
            pltpu.SemaphoreType.DMA((2,)),
            pltpu.SemaphoreType.DMA((2,)),
        ],
        compiler_params=pltpu.CompilerParams(
            collective_id=0, has_side_effects=True, vmem_limit_bytes=32 << 20
        ),
        name="exchange",
    )(xyz, pot, cand, home)


def finish_kernel(
    low, own, high, dual, pot, target, dual_pot, moments, new_pot,
    above_in, below_in, got, dual_send, dual_recv, send_sem, recv_sem,
):
    x, g = lax.axis_index("gx"), lax.axis_index("gy")
    below, above = (x + N_GX - 1) % N_GX, (x + 1) % N_GX
    others = [(g + d) % N_GY for d in range(1, N_GY)]
    meet([(below, g), (above, g)] + [(x, peer) for peer in others])
    down = pltpu.make_async_remote_copy(
        low, above_in, send_sem.at[0], recv_sem.at[0], device_id=(below, g), device_id_type=MESH
    )
    up = pltpu.make_async_remote_copy(
        high, below_in, send_sem.at[1], recv_sem.at[1], device_id=(above, g), device_id_type=MESH
    )
    down.start()
    up.start()
    copies = []
    for d, peer in enumerate(others):
        copy = pltpu.make_async_remote_copy(
            dual.at[peer], got.at[g], dual_send.at[d], dual_recv.at[d],
            device_id=(x, peer), device_id_type=MESH,
        )
        copy.start()
        copies.append(copy)
    got[g] = dual[g]
    for copy in copies:
        copy.wait()
    row = lax.broadcasted_iota(jnp.int32, (ROWS, BS), 0).astype(jnp.float32)
    total = None
    for half in range(2):
        fill = None
        for j in range(4):
            index = got[4 * half + j, PAIR_CAP : PAIR_CAP + 1, :]
            fill = index if fill is None else jnp.maximum(fill, index)
        hot = bf(jnp.where(row == fill, 1.0, 0.0))
        rest = jnp.concatenate([got[4 * half + j, :PAIR_CAP, :] for j in range(4)], axis=0)
        for _ in range(3):
            piece = bf(rest)
            rest = rest - f32(piece)
            term = jnp.dot(hot, piece, preferred_element_type=jnp.float32)
            total = term if total is None else total + term
    dual_pot[...] = total
    down.wait()
    up.wait()

    @pl.loop(0, SB // 16)
    def _(i):
        at = pl.multiple_of(i * 64, 64)
        moments[pl.ds(at, 64), :] = (
            own[pl.ds(at, 64), :] + above_in[pl.ds(at, 64), :] + below_in[pl.ds(at, 64), :]
        )
        for j in range(2):
            rows = pl.ds(pl.multiple_of(i * 16, 16) + 8 * j, 8)
            mass = moments[pl.ds(at + 32 * j, 8, stride=4), :]
            new_pot[rows, :] = pot[rows, :] + STEP * (target[rows, :] - mass)


def finish(low, own, high, dual, pot, target):
    return pl.pallas_call(
        finish_kernel,
        in_specs=[VMEM] * 6,
        out_specs=[VMEM] * 3,
        out_shape=[
            jax.ShapeDtypeStruct((ROWS, BS), jnp.float32),
            jax.ShapeDtypeStruct((4 * SB, BS), jnp.float32),
            jax.ShapeDtypeStruct((SB, BS), jnp.float32),
        ],
        scratch_shapes=[
            pltpu.VMEM((4 * SB, BS), jnp.float32),
            pltpu.VMEM((4 * SB, BS), jnp.float32),
            pltpu.VMEM((N_GY, GROUP, BS), jnp.float32),
            pltpu.SemaphoreType.DMA((N_GY - 1,)),
            pltpu.SemaphoreType.DMA((N_GY - 1,)),
            pltpu.SemaphoreType.DMA((2,)),
            pltpu.SemaphoreType.DMA((2,)),
        ],
        compiler_params=pltpu.CompilerParams(
            collective_id=1, has_side_effects=True, vmem_limit_bytes=32 << 20
        ),
        name="finish",
    )(low, own, high, dual, pot, target)


BUFFERS = ("split", "xat", "part", "top", "f8")


def work_kernel(
    pidx, plan, vox, mass, low_in, own_in, high_in,
    low_out, own_out, high_out, dual, mom, ypool, order, place, ranks, *scratch,
):
    first_lane = (lax.axis_index("gy") & 3) * PAIR_CAP
    for g in range(N_GY):
        ranks[g] = 0

    def compact(h, n):
        for u in range(2):
            v = 2 * h + u
            p = plan[v]
            occupied = (p >= 0).astype(jnp.int32)
            dest = (p >> 7) & 7
            rank = ranks[dest]
            ranks[dest] = rank + occupied
            order[n] = v
            place[n] = (dest << 16) | (rank << 8) | (p & 127)
            n = n + occupied
        return n

    n = lax.fori_loop(0, VB // 2, compact, jnp.int32(0))
    size = len(BUFFERS)
    bufs = [dict(zip(BUFFERS, scratch[i * size : (i + 1) * size])) for i in range(SLOTS * TOGETHER)]
    sub = lax.broadcasted_iota(jnp.int32, (8, BS), 0)
    low = sub < 4
    lane = lax.broadcasted_iota(jnp.int32, (1, BS), 1)
    dual[...] = jnp.full(dual.shape, -1.0, jnp.float32)
    for q, table in enumerate((low_in, own_in, high_in)):

        @pl.loop(0, SB // 16)
        def _(g):
            for j in range(16):
                i = g * 16 + j
                t = table[pl.ds(i, 4, stride=SB), :]
                a = jnp.concatenate([t, t], axis=0)
                hi = f32(bf(a))
                mid = f32(bf(a - hi))
                first = jnp.where(low, hi, mid)
                second = jnp.where(sub == 3, a - hi - mid, jnp.where(sub == 7, 1.0, first))
                ypool[q * SB + i] = bf(jnp.concatenate([first, second], axis=0))
                mom[q * SB + i] = jnp.zeros((8, BS), jnp.float32)

    def prepare(t, b):
        s = order[t]
        x = vox[pl.ds(s, 3, stride=VB), :] - 0.5
        xh = f32(bf(x))
        xl = x - xh
        tops = [f32(ypool[pidx[s * KC + k], 0:8, :]) for k in range(KC)]
        while len(tops) > 1:
            tops = [jnp.maximum(a, c) for a, c in zip(tops[::2], tops[1::2])]
        top = jnp.max(tops[0][3:4], axis=1, keepdims=True)
        top = jnp.broadcast_to(top, (1, BS))
        one = jnp.ones((1, BS), jnp.float32)
        xa = jnp.concatenate([xh, one, xh, one, xl, one, xl, -top], axis=0)
        b["xat"][...] = bf(xa.T)
        b["top"][0:1, :] = top

    def weigh_and_spread(t, b, told, bold):
        part = None
        s = order[t] if t is not None else None
        sold = order[told] if told is not None else None
        for c in range(KC // 2):
            if t is not None:
                y = [ypool[pidx[s * KC + 2 * c + j]] for j in range(2)]
                sc = jnp.dot(
                    b["xat"][...],
                    jnp.concatenate(y, axis=1),
                    preferred_element_type=jnp.float32,
                )
            if told is not None:
                e2 = jnp.concatenate([bold["split"][2 * c], bold["split"][2 * c + 1]], axis=1)
                m = jnp.dot(bold["f8"][...], e2, preferred_element_type=jnp.float32)
                for j in range(2):
                    mom[pidx[sold * KC + 2 * c + j]] += m[:, j * BS : (j + 1) * BS]
            if t is not None:
                e = jnp.exp2(sc)
                eh = bf(e)
                el = bf(e - f32(eh))
                for j in range(2):
                    b["split"][2 * c + j, 0:BS, :] = eh[:, j * BS : (j + 1) * BS]
                    b["split"][2 * c + j, BS:, :] = el[:, j * BS : (j + 1) * BS]
                p = e[:, :BS] + e[:, BS:]
                part = p if part is None else part + p
        if t is not None:
            b["part"][...] = part

    def norm(t, b):
        s = order[t]
        d = jnp.sum(b["part"][...].T, axis=0, keepdims=True)
        xr = vox[pl.ds(s, 3, stride=VB), :]
        x = xr - 0.5
        sq = jnp.sum(x * x, axis=0, keepdims=True)
        where = place[t]
        top_row = (where >> 16) * GROUP
        rank = (where >> 8) & 255
        mark = pl.ds(top_row + PAIR_CAP, 1)
        dual[mark, :] = jnp.where(
            lane == first_lane + rank, (where & 255).astype(jnp.float32), dual[mark, :]
        )
        dual[pl.ds(top_row + rank, 1), :] = (1.0 / EPS) * sq - LN2 * (b["top"][0:1, :] + jnp.log2(d))
        w = mass[pl.ds(s, 1), :] / d
        f = jnp.concatenate([w, xr * w], axis=0)
        fh = f32(bf(f))
        f8 = bf(jnp.concatenate([fh, f - fh], axis=0))
        b["f8"][...] = jnp.concatenate([f8, f8], axis=1)

    def step(g, slot, valid):
        for stage in range(3):
            for u in range(TOGETHER):
                at = lambda lag: (g - lag) * TOGETHER + u if valid(lag) else None
                buf = lambda lag: bufs[((slot - lag) % SLOTS) * TOGETHER + u]
                if stage == 0 and valid(0):
                    prepare(at(0), buf(0))
                if stage == 1 and (valid(1) or valid(3)):
                    weigh_and_spread(at(1), buf(1), at(3), buf(3))
                if stage == 2 and valid(2):
                    norm(at(2), buf(2))

    groups = n // TOGETHER

    @pl.when(n > 0)
    def _():
        for g in range(SLOTS):
            step(g, g, lambda lag: lag <= g)

        @pl.loop(0, (groups - SLOTS) // SLOTS)
        def _(h):
            for u in range(SLOTS):
                step(SLOTS + SLOTS * h + u, u, lambda lag: True)

        for e in range(3):
            step(groups + e, e, lambda lag: lag > e)

    for q, out in enumerate((low_out, own_out, high_out)):

        @pl.loop(0, SB // 16)
        def _(g):
            for j in range(16):
                m = mom[q * SB + g * 16 + j]
                out[g * 16 + j] = m[0:4] + m[4:8]


def work(pidx, plan, vox, mass, low, own, high):
    moments = jax.ShapeDtypeStruct((SB, 4, BS), jnp.float32)
    scratch = [
        pltpu.VMEM((POOL, 8, BS), jnp.float32),
        pltpu.VMEM((POOL, 16, BS), jnp.bfloat16),
        pltpu.SMEM((VB + 8,), jnp.int32),
        pltpu.SMEM((VB + 8,), jnp.int32),
        pltpu.SMEM((N_GY,), jnp.int32),
    ]
    scratch += [
        pltpu.VMEM((KC, 2 * BS, BS), jnp.bfloat16),
        pltpu.VMEM((BS, 16), jnp.bfloat16),
        pltpu.VMEM((BS, BS), jnp.float32),
        pltpu.VMEM((8, BS), jnp.float32),
        pltpu.VMEM((8, 2 * BS), jnp.bfloat16),
    ] * (SLOTS * TOGETHER)
    return pl.pallas_call(
        work_kernel,
        in_specs=[SMEM] * 2 + [VMEM] * 5,
        out_specs=[VMEM] * 4,
        out_shape=[moments] * 3 + [jax.ShapeDtypeStruct((N_GY * GROUP, BS), jnp.float32)],
        scratch_shapes=scratch,
        compiler_params=pltpu.CompilerParams(vmem_limit_bytes=56 << 20),
        name="work",
    )(pidx, plan, vox, mass, low, own, high)


def on_device(
    voxel_xyz, voxel_mass, candidates, offload_plan, seed_xyz, seed_pot, seed_target, seed_home
):
    own_in, low_in, high_in, pidx = exchange(
        jnp.transpose(seed_xyz, (1, 0, 2)), seed_pot, candidates.T, seed_home
    )
    vox = jnp.transpose(voxel_xyz, (1, 0, 2)).reshape(3 * VB, BS)
    low, own, high, dual = work(pidx, offload_plan, vox, voxel_mass, low_in, own_in, high_in)
    flat = lambda m: m.reshape(4 * SB, BS)
    dual_pot, moments, new_pot = finish(
        flat(low), flat(own), flat(high), dual.reshape(N_GY, GROUP, BS), seed_pot, seed_target
    )
    return (dual_pot, moments.reshape(SB, 4, BS), new_pot)


def solution(mesh):
    return jax.shard_map(
        on_device,
        mesh=mesh,
        in_specs=(
            P(("gx", "gy"), None, None),
            P(("gx", "gy"), None),
            P(("gx", "gy"), None),
            P(("gx", "gy")),
            P(("gx", "gy"), None, None),
            P(("gx", "gy"), None),
            P(("gx", "gy"), None),
            P(),
        ),
        out_specs=(P(("gx", "gy"), None), P(("gx", "gy"), None, None), P(("gx", "gy"), None)),
        check_vma=False,
    )
```

```python
import math

import jax
import jax.numpy as jnp
from jax import lax
from jax.experimental import pallas as pl
from jax.experimental.pallas import tpu as pltpu
from jax.sharding import PartitionSpec as P

BS = 128
KC = 8
PAIR_CAP = 32
VB = 256
SB = 512
POOL = 3 * SB
N_GX = 16
N_GY = 8
ROWS = 128
GROUP = 40
SLOTS = 4
TOGETHER = 2

EPS = 0.05
STEP = 0.5
LOG2E = math.log2(math.e)
LN2 = math.log(2.0)

VMEM = pl.BlockSpec(memory_space=pltpu.VMEM)
SMEM = pl.BlockSpec(memory_space=pltpu.SMEM)
HBM = pl.BlockSpec(memory_space=pltpu.HBM)
MESH = pl.DeviceIdType.MESH


def bf(x):
    return x.astype(jnp.bfloat16)


def f32(x):
    return x.astype(jnp.float32)


def meet(peers):
    barrier = pltpu.get_barrier_semaphore()
    for peer in peers:
        pl.semaphore_signal(barrier, inc=1, device_id=peer, device_id_type=MESH)
    pl.semaphore_wait(barrier, len(peers))


def exchange_kernel(
    xyz_hbm, pot_hbm, cand_hbm, home_hbm, own, low, high, pidx,
    xyz, pot, cand, home, load_sem, send_sem, recv_sem,
):
    x, g = lax.axis_index("gx"), lax.axis_index("gy")
    below, above = (x + N_GX - 1) % N_GX, (x + 1) % N_GX
    pairs = ((xyz_hbm, xyz), (pot_hbm, pot), (cand_hbm, cand), (home_hbm, home))
    loads = [pltpu.make_async_copy(a, b, load_sem.at[i]) for i, (a, b) in enumerate(pairs)]
    for load in loads:
        load.start()
    loads[0].wait()
    loads[1].wait()

    @pl.loop(0, SB // 64)
    def _(i):
        at = pl.multiple_of(i * 64, 64)
        square = None
        for c in range(3):
            y = xyz[c, pl.ds(at, 64), :] - 0.5
            own[pl.ds(c * SB + at, 64), :] = (2.0 * LOG2E / EPS) * y
            square = y * y if square is None else square + y * y
        own[pl.ds(3 * SB + at, 64), :] = LOG2E * (pot[pl.ds(at, 64), :] - (1.0 / EPS) * square)

    meet([(below, g), (above, g)])
    up = pltpu.make_async_remote_copy(
        own, low, send_sem.at[0], recv_sem.at[0], device_id=(above, g), device_id_type=MESH
    )
    down = pltpu.make_async_remote_copy(
        own, high, send_sem.at[1], recv_sem.at[1], device_id=(below, g), device_id_type=MESH
    )
    up.start()
    down.start()
    loads[2].wait()
    loads[3].wait()

    @pl.loop(0, VB // 2)
    def _(h):
        for u in range(2):
            v = 2 * h + u
            for k in range(KC):
                s = home[cand[k, v]]
                pidx[v * KC + k] = ((((s >> 12) - x + 1) & 15) << 9) | (s & 511)

    up.wait()
    down.wait()


def exchange(xyz, pot, cand, home):
    table = jax.ShapeDtypeStruct((4 * SB, BS), jnp.float32)
    return pl.pallas_call(
        exchange_kernel,
        in_specs=[HBM] * 4,
        out_specs=[VMEM] * 3 + [SMEM],
        out_shape=[table] * 3 + [jax.ShapeDtypeStruct((VB * KC,), jnp.int32)],
        scratch_shapes=[
            pltpu.VMEM((3, SB, BS), jnp.float32),
            pltpu.VMEM((SB, BS), jnp.float32),
            pltpu.SMEM((KC, VB), jnp.int32),
            pltpu.SMEM((N_GX * N_GY * SB,), jnp.int32),
            pltpu.SemaphoreType.DMA((4,)),
            pltpu.SemaphoreType.DMA((2,)),
            pltpu.SemaphoreType.DMA((2,)),
        ],
        compiler_params=pltpu.CompilerParams(
            collective_id=0, has_side_effects=True, vmem_limit_bytes=16 << 20
        ),
        name="exchange",
    )(*(pltpu.with_memory_space_constraint(a, pltpu.HBM) for a in (xyz, pot, cand, home)))


def deliver_kernel(
    low, high, dual, above_in, below_in, got, dual_send, dual_recv, send_sem, recv_sem, own_sem
):
    x, g = lax.axis_index("gx"), lax.axis_index("gy")
    below, above = (x + N_GX - 1) % N_GX, (x + 1) % N_GX
    others = [(g + d) % N_GY for d in range(1, N_GY)]
    meet([(below, g), (above, g)] + [(x, peer) for peer in others])
    copies = [
        pltpu.make_async_remote_copy(
            low, above_in, send_sem.at[0], recv_sem.at[0],
            device_id=(below, g), device_id_type=MESH,
        ),
        pltpu.make_async_remote_copy(
            high, below_in, send_sem.at[1], recv_sem.at[1],
            device_id=(above, g), device_id_type=MESH,
        ),
    ]
    for d, peer in enumerate(others):
        copies.append(
            pltpu.make_async_remote_copy(
                dual.at[peer], got.at[g], dual_send.at[d], dual_recv.at[d],
                device_id=(x, peer), device_id_type=MESH,
            )
        )
    keep = pltpu.make_async_copy(dual.at[g], got.at[g], own_sem)
    for copy in copies:
        copy.start()
    keep.start()
    keep.wait()
    for copy in copies:
        copy.wait()


def deliver(low, high, dual):
    moments = jax.ShapeDtypeStruct((4 * SB, BS), jnp.float32)
    return pl.pallas_call(
        deliver_kernel,
        in_specs=[VMEM] * 3,
        out_specs=[VMEM] * 3,
        out_shape=[moments] * 2 + [jax.ShapeDtypeStruct((N_GY, GROUP, BS), jnp.float32)],
        scratch_shapes=[
            pltpu.SemaphoreType.DMA((N_GY - 1,)),
            pltpu.SemaphoreType.DMA((N_GY - 1,)),
            pltpu.SemaphoreType.DMA((2,)),
            pltpu.SemaphoreType.DMA((2,)),
            pltpu.SemaphoreType.DMA(()),
        ],
        compiler_params=pltpu.CompilerParams(
            collective_id=1, has_side_effects=True, vmem_limit_bytes=16 << 20
        ),
        name="deliver",
    )(low, high, dual)


def total_kernel(
    own, above_in, below_in, got, pot, target, dual_hbm, moments_hbm, new_pot_hbm,
    moments, new_pot, dual_pot, sems,
):
    parts = 4
    size = 4 * SB // parts
    sends = []
    for q in range(parts):

        @pl.loop(0, SB // 16 // parts)
        def _(i):
            at = pl.multiple_of(q * size + i * 64, 64)
            moments[pl.ds(at, 64), :] = (
                own[pl.ds(at, 64), :] + above_in[pl.ds(at, 64), :] + below_in[pl.ds(at, 64), :]
            )
            for j in range(2):
                rows = pl.ds(pl.multiple_of(q * (size // 4) + i * 16, 16) + 8 * j, 8)
                mass = moments[pl.ds(at + 32 * j, 8, stride=4), :]
                new_pot[rows, :] = pot[rows, :] + STEP * (target[rows, :] - mass)

        some = pl.ds(q * size, size)
        sends.append(pltpu.make_async_copy(moments.at[some], moments_hbm.at[some], sems.at[q]))
        sends[-1].start()
    sends.append(pltpu.make_async_copy(new_pot, new_pot_hbm, sems.at[parts]))
    sends[-1].start()
    row = lax.broadcasted_iota(jnp.int32, (ROWS, BS), 0).astype(jnp.float32)
    total = None
    for half in range(2):
        fill = None
        for j in range(4):
            index = got[4 * half + j, PAIR_CAP : PAIR_CAP + 1, :]
            fill = index if fill is None else jnp.maximum(fill, index)
        hot = bf(jnp.where(row == fill, 1.0, 0.0))
        rest = jnp.concatenate([got[4 * half + j, :PAIR_CAP, :] for j in range(4)], axis=0)
        for _ in range(3):
            piece = bf(rest)
            rest = rest - f32(piece)
            term = jnp.dot(hot, piece, preferred_element_type=jnp.float32)
            total = term if total is None else total + term
    dual_pot[...] = total
    sends.append(pltpu.make_async_copy(dual_pot, dual_hbm, sems.at[parts + 1]))
    sends[-1].start()
    for send in sends:
        send.wait()


def total(own, above_in, below_in, got, pot, target):
    shapes = [(ROWS, BS), (4 * SB, BS), (SB, BS)]
    return pl.pallas_call(
        total_kernel,
        in_specs=[VMEM] * 6,
        out_specs=[HBM] * 3,
        out_shape=[jax.ShapeDtypeStruct(shape, jnp.float32) for shape in shapes],
        scratch_shapes=[
            pltpu.VMEM((4 * SB, BS), jnp.float32),
            pltpu.VMEM((SB, BS), jnp.float32),
            pltpu.VMEM((ROWS, BS), jnp.float32),
            pltpu.SemaphoreType.DMA((6,)),
        ],
        compiler_params=pltpu.CompilerParams(vmem_limit_bytes=16 << 20),
        name="total",
    )(own, above_in, below_in, got, pot, target)


BUFFERS = ("split", "xat", "part", "top", "f8")


def work_kernel(
    pidx, plan, vox, mass, low_in, own_in, high_in,
    low_out, own_out, high_out, dual, mom, ypool, order, place, ranks, *scratch,
):
    first_lane = (lax.axis_index("gy") & 3) * PAIR_CAP
    for g in range(N_GY):
        ranks[g] = 0

    def compact(h, n):
        for u in range(2):
            v = 2 * h + u
            p = plan[v]
            occupied = (p >= 0).astype(jnp.int32)
            dest = (p >> 7) & 7
            rank = ranks[dest]
            ranks[dest] = rank + occupied
            order[n] = v
            place[n] = (dest << 16) | (rank << 8) | (p & 127)
            n = n + occupied
        return n

    n = lax.fori_loop(0, VB // 2, compact, jnp.int32(0))
    size = len(BUFFERS)
    bufs = [dict(zip(BUFFERS, scratch[i * size : (i + 1) * size])) for i in range(SLOTS * TOGETHER)]
    sub = lax.broadcasted_iota(jnp.int32, (8, BS), 0)
    low = sub < 4
    lane = lax.broadcasted_iota(jnp.int32, (1, BS), 1)
    dual[...] = jnp.full(dual.shape, -1.0, jnp.float32)
    for q, table in enumerate((low_in, own_in, high_in)):

        @pl.loop(0, SB // 16)
        def _(g):
            for j in range(16):
                i = g * 16 + j
                t = table[pl.ds(i, 4, stride=SB), :]
                a = jnp.concatenate([t, t], axis=0)
                hi = f32(bf(a))
                mid = f32(bf(a - hi))
                first = jnp.where(low, hi, mid)
                second = jnp.where(sub == 3, a - hi - mid, jnp.where(sub == 7, 1.0, first))
                ypool[q * SB + i] = bf(jnp.concatenate([first, second], axis=0))
                mom[q * SB + i] = jnp.zeros((8, BS), jnp.float32)

    def prepare(t, b):
        s = order[t]
        x = vox[pl.ds(s, 3, stride=VB), :] - 0.5
        xh = f32(bf(x))
        xl = x - xh
        tops = [f32(ypool[pidx[s * KC + k], 0:8, :]) for k in range(KC)]
        while len(tops) > 1:
            tops = [jnp.maximum(a, c) for a, c in zip(tops[::2], tops[1::2])]
        top = jnp.max(tops[0][3:4], axis=1, keepdims=True)
        top = jnp.broadcast_to(top, (1, BS))
        one = jnp.ones((1, BS), jnp.float32)
        xa = jnp.concatenate([xh, one, xh, one, xl, one, xl, -top], axis=0)
        b["xat"][...] = bf(xa.T)
        b["top"][0:1, :] = top

    def weigh_and_spread(t, b, told, bold):
        part = None
        s = order[t] if t is not None else None
        sold = order[told] if told is not None else None
        for c in range(KC // 2):
            if t is not None:
                y = [ypool[pidx[s * KC + 2 * c + j]] for j in range(2)]
                sc = jnp.dot(
                    b["xat"][...],
                    jnp.concatenate(y, axis=1),
                    preferred_element_type=jnp.float32,
                )
            if told is not None:
                e2 = jnp.concatenate([bold["split"][2 * c], bold["split"][2 * c + 1]], axis=1)
                m = jnp.dot(bold["f8"][...], e2, preferred_element_type=jnp.float32)
                for j in range(2):
                    mom[pidx[sold * KC + 2 * c + j]] += m[:, j * BS : (j + 1) * BS]
            if t is not None:
                e = jnp.exp2(sc)
                eh = bf(e)
                el = bf(e - f32(eh))
                for j in range(2):
                    b["split"][2 * c + j, 0:BS, :] = eh[:, j * BS : (j + 1) * BS]
                    b["split"][2 * c + j, BS:, :] = el[:, j * BS : (j + 1) * BS]
                p = e[:, :BS] + e[:, BS:]
                part = p if part is None else part + p
        if t is not None:
            b["part"][...] = part

    def norm(t, b):
        s = order[t]
        d = jnp.sum(b["part"][...].T, axis=0, keepdims=True)
        xr = vox[pl.ds(s, 3, stride=VB), :]
        x = xr - 0.5
        sq = jnp.sum(x * x, axis=0, keepdims=True)
        where = place[t]
        top_row = (where >> 16) * GROUP
        rank = (where >> 8) & 255
        mark = pl.ds(top_row + PAIR_CAP, 1)
        dual[mark, :] = jnp.where(
            lane == first_lane + rank, (where & 255).astype(jnp.float32), dual[mark, :]
        )
        dual[pl.ds(top_row + rank, 1), :] = (1.0 / EPS) * sq - LN2 * (b["top"][0:1, :] + jnp.log2(d))
        w = mass[pl.ds(s, 1), :] / d
        f = jnp.concatenate([w, xr * w], axis=0)
        fh = f32(bf(f))
        f8 = bf(jnp.concatenate([fh, f - fh], axis=0))
        b["f8"][...] = jnp.concatenate([f8, f8], axis=1)

    def step(g, slot, valid):
        for stage in range(3):
            for u in range(TOGETHER):
                at = lambda lag: (g - lag) * TOGETHER + u if valid(lag) else None
                buf = lambda lag: bufs[((slot - lag) % SLOTS) * TOGETHER + u]
                if stage == 0 and valid(0):
                    prepare(at(0), buf(0))
                if stage == 1 and (valid(1) or valid(3)):
                    weigh_and_spread(at(1), buf(1), at(3), buf(3))
                if stage == 2 and valid(2):
                    norm(at(2), buf(2))

    groups = n // TOGETHER

    @pl.when(n > 0)
    def _():
        for g in range(SLOTS):
            step(g, g, lambda lag: lag <= g)

        @pl.loop(0, (groups - SLOTS) // SLOTS)
        def _(h):
            for u in range(SLOTS):
                step(SLOTS + SLOTS * h + u, u, lambda lag: True)

        for e in range(3):
            step(groups + e, e, lambda lag: lag > e)

    for q, out in enumerate((low_out, own_out, high_out)):

        @pl.loop(0, SB // 16)
        def _(g):
            for j in range(16):
                m = mom[q * SB + g * 16 + j]
                out[g * 16 + j] = m[0:4] + m[4:8]


def work(pidx, plan, vox, mass, low, own, high):
    moments = jax.ShapeDtypeStruct((SB, 4, BS), jnp.float32)
    scratch = [
        pltpu.VMEM((POOL, 8, BS), jnp.float32),
        pltpu.VMEM((POOL, 16, BS), jnp.bfloat16),
        pltpu.SMEM((VB + 8,), jnp.int32),
        pltpu.SMEM((VB + 8,), jnp.int32),
        pltpu.SMEM((N_GY,), jnp.int32),
    ]
    scratch += [
        pltpu.VMEM((KC, 2 * BS, BS), jnp.bfloat16),
        pltpu.VMEM((BS, 16), jnp.bfloat16),
        pltpu.VMEM((BS, BS), jnp.float32),
        pltpu.VMEM((8, BS), jnp.float32),
        pltpu.VMEM((8, 2 * BS), jnp.bfloat16),
    ] * (SLOTS * TOGETHER)
    return pl.pallas_call(
        work_kernel,
        in_specs=[SMEM] * 2 + [VMEM] * 5,
        out_specs=[VMEM] * 4,
        out_shape=[moments] * 3 + [jax.ShapeDtypeStruct((N_GY * GROUP, BS), jnp.float32)],
        scratch_shapes=scratch,
        compiler_params=pltpu.CompilerParams(vmem_limit_bytes=32 << 20),
        name="work",
    )(pidx, plan, vox, mass, low, own, high)


def on_device(
    voxel_xyz, voxel_mass, candidates, offload_plan, seed_xyz, seed_pot, seed_target, seed_home
):
    own_in, low_in, high_in, pidx = exchange(
        jnp.transpose(seed_xyz, (1, 0, 2)), seed_pot, candidates.T, seed_home
    )
    vox = jnp.transpose(voxel_xyz, (1, 0, 2)).reshape(3 * VB, BS)
    low, own, high, dual = work(pidx, offload_plan, vox, voxel_mass, low_in, own_in, high_in)
    flat = lambda m: m.reshape(4 * SB, BS)
    above_in, below_in, got = deliver(flat(low), flat(high), dual.reshape(N_GY, GROUP, BS))
    dual_pot, moments, new_pot = total(
        flat(own), above_in, below_in, got, seed_pot, seed_target
    )
    return (dual_pot, moments.reshape(SB, 4, BS), new_pot)


def solution(mesh):
    return jax.shard_map(
        on_device,
        mesh=mesh,
        in_specs=(
            P(("gx", "gy"), None, None),
            P(("gx", "gy"), None),
            P(("gx", "gy"), None),
            P(("gx", "gy")),
            P(("gx", "gy"), None, None),
            P(("gx", "gy"), None),
            P(("gx", "gy"), None),
            P(),
        ),
        out_specs=(P(("gx", "gy"), None), P(("gx", "gy"), None, None), P(("gx", "gy"), None)),
        check_vma=False,
    )
```

```python
import math

import jax
import jax.numpy as jnp
from jax import lax
from jax.experimental import pallas as pl
from jax.experimental.pallas import tpu as pltpu
from jax.sharding import PartitionSpec as P

BS = 128
KC = 8
PAIR_CAP = 32
VB = 256
SB = 512
POOL = 3 * SB
N_GX = 16
N_GY = 8
ROWS = 128
GROUP = 40
SLOTS = 4
TOGETHER = 2
CHUNKS = 4

EPS = 0.05
STEP = 0.5
LOG2E = math.log2(math.e)
LN2 = math.log(2.0)

VMEM = pl.BlockSpec(memory_space=pltpu.VMEM)
SMEM = pl.BlockSpec(memory_space=pltpu.SMEM)
HBM = pl.BlockSpec(memory_space=pltpu.HBM)
MESH = pl.DeviceIdType.MESH


def bf(x):
    return x.astype(jnp.bfloat16)


def f32(x):
    return x.astype(jnp.float32)


def meet(peers):
    barrier = pltpu.get_barrier_semaphore()
    for peer in peers:
        pl.semaphore_signal(barrier, inc=1, device_id=peer, device_id_type=MESH)
    pl.semaphore_wait(barrier, len(peers))


def exchange_kernel(
    xyz_hbm, pot_hbm, cand_hbm, home_hbm, ypool, pidx,
    xyz, pot, plane, cand, home, load_sem, send_sem, recv_sem,
):
    x, g = lax.axis_index("gx"), lax.axis_index("gy")
    below, above = (x + N_GX - 1) % N_GX, (x + 1) % N_GX
    pairs = (
        (xyz_hbm, xyz.at[1]), (pot_hbm, pot.at[1]), (cand_hbm, cand), (home_hbm, home)
    )
    loads = [pltpu.make_async_copy(a, b, load_sem.at[i]) for i, (a, b) in enumerate(pairs)]
    for load in loads:
        load.start()
    meet([(below, g), (above, g)])
    copies = []
    for q in range(CHUNKS):
        some = pl.ds(q * (SB // CHUNKS), SB // CHUNKS)
        for way, (slot, peer) in enumerate(((0, above), (2, below))):
            for kind, (source, dest) in enumerate(
                (
                    (xyz_hbm.at[:, some, :], xyz.at[slot, :, some, :]),
                    (pot_hbm.at[some, :], pot.at[slot, some, :]),
                )
            ):
                i = (q * 2 + way) * 2 + kind
                copy = pltpu.make_async_remote_copy(
                    source, dest, send_sem.at[i], recv_sem.at[i],
                    device_id=(peer, g), device_id_type=MESH,
                )
                copy.start()
                copies.append(copy)

    sub = lax.broadcasted_iota(jnp.int32, (8, BS), 0)
    low = sub < 4

    def build(slot, start, count):
        @pl.loop(0, count // 16)
        def _(i):
            at = pl.multiple_of(start + i * 16, 16)
            square = None
            for c in range(3):
                y = xyz[slot, c, pl.ds(at, 16), :] - 0.5
                plane[c * 16 : (c + 1) * 16, :] = (2.0 * LOG2E / EPS) * y
                square = y * y if square is None else square + y * y
            plane[48:64, :] = LOG2E * (pot[slot, pl.ds(at, 16), :] - (1.0 / EPS) * square)
            for j in range(16):
                t = plane[pl.ds(j, 4, stride=16), :]
                a = jnp.concatenate([t, t], axis=0)
                hi = f32(bf(a))
                mid = f32(bf(a - hi))
                first = jnp.where(low, hi, mid)
                second = jnp.where(sub == 3, a - hi - mid, jnp.where(sub == 7, 1.0, first))
                ypool[slot * SB + at + j] = bf(jnp.concatenate([first, second], axis=0))

    loads[0].wait()
    loads[1].wait()
    build(1, 0, SB)
    loads[2].wait()
    loads[3].wait()

    @pl.loop(0, VB // 2)
    def _(h):
        for u in range(2):
            v = 2 * h + u
            for k in range(KC):
                s = home[cand[k, v]]
                pidx[v * KC + k] = ((((s >> 12) - x + 1) & 15) << 9) | (s & 511)

    for q in range(CHUNKS):
        for copy in copies[4 * q : 4 * q + 4]:
            copy.wait_recv()
        for slot in (0, 2):
            build(slot, q * (SB // CHUNKS), SB // CHUNKS)
    for copy in copies:
        copy.wait_send()


def exchange(xyz, pot, cand, home):
    return pl.pallas_call(
        exchange_kernel,
        in_specs=[HBM] * 4,
        out_specs=[VMEM, SMEM],
        out_shape=[
            jax.ShapeDtypeStruct((POOL, 16, BS), jnp.bfloat16),
            jax.ShapeDtypeStruct((VB * KC,), jnp.int32),
        ],
        scratch_shapes=[
            pltpu.VMEM((3, 3, SB, BS), jnp.float32),
            pltpu.VMEM((3, SB, BS), jnp.float32),
            pltpu.VMEM((64, BS), jnp.float32),
            pltpu.SMEM((KC, VB), jnp.int32),
            pltpu.SMEM((N_GX * N_GY * SB,), jnp.int32),
            pltpu.SemaphoreType.DMA((4,)),
            pltpu.SemaphoreType.DMA((4 * CHUNKS,)),
            pltpu.SemaphoreType.DMA((4 * CHUNKS,)),
        ],
        compiler_params=pltpu.CompilerParams(
            collective_id=0, has_side_effects=True, vmem_limit_bytes=16 << 20
        ),
        name="exchange",
    )(*(pltpu.with_memory_space_constraint(a, pltpu.HBM) for a in (xyz, pot, cand, home)))


def deliver_kernel(
    low, high, dual, above_in, below_in, got, dual_send, dual_recv, send_sem, recv_sem, own_sem
):
    x, g = lax.axis_index("gx"), lax.axis_index("gy")
    below, above = (x + N_GX - 1) % N_GX, (x + 1) % N_GX
    others = [(g + d) % N_GY for d in range(1, N_GY)]
    meet([(below, g), (above, g)] + [(x, peer) for peer in others])
    copies = [
        pltpu.make_async_remote_copy(
            low, above_in, send_sem.at[0], recv_sem.at[0],
            device_id=(below, g), device_id_type=MESH,
        ),
        pltpu.make_async_remote_copy(
            high, below_in, send_sem.at[1], recv_sem.at[1],
            device_id=(above, g), device_id_type=MESH,
        ),
    ]
    for d, peer in enumerate(others):
        copies.append(
            pltpu.make_async_remote_copy(
                dual.at[peer], got.at[g], dual_send.at[d], dual_recv.at[d],
                device_id=(x, peer), device_id_type=MESH,
            )
        )
    keep = pltpu.make_async_copy(dual.at[g], got.at[g], own_sem)
    for copy in copies:
        copy.start()
    keep.start()
    keep.wait()
    for copy in copies:
        copy.wait()


def deliver(low, high, dual):
    moments = jax.ShapeDtypeStruct((4 * SB, BS), jnp.float32)
    return pl.pallas_call(
        deliver_kernel,
        in_specs=[VMEM] * 3,
        out_specs=[VMEM] * 3,
        out_shape=[moments] * 2 + [jax.ShapeDtypeStruct((N_GY, GROUP, BS), jnp.float32)],
        scratch_shapes=[
            pltpu.SemaphoreType.DMA((N_GY - 1,)),
            pltpu.SemaphoreType.DMA((N_GY - 1,)),
            pltpu.SemaphoreType.DMA((2,)),
            pltpu.SemaphoreType.DMA((2,)),
            pltpu.SemaphoreType.DMA(()),
        ],
        compiler_params=pltpu.CompilerParams(
            collective_id=1, has_side_effects=True, vmem_limit_bytes=16 << 20
        ),
        name="deliver",
    )(low, high, dual)


def total_kernel(
    own, above_in, below_in, got, pot, target, dual_hbm, moments_hbm, new_pot_hbm,
    moments, new_pot, dual_pot, sems,
):
    parts = 4
    size = 4 * SB // parts
    sends = []
    for q in range(parts):

        @pl.loop(0, SB // 16 // parts)
        def _(i):
            at = pl.multiple_of(q * size + i * 64, 64)
            moments[pl.ds(at, 64), :] = (
                own[pl.ds(at, 64), :] + above_in[pl.ds(at, 64), :] + below_in[pl.ds(at, 64), :]
            )
            for j in range(2):
                rows = pl.ds(pl.multiple_of(q * (size // 4) + i * 16, 16) + 8 * j, 8)
                mass = moments[pl.ds(at + 32 * j, 8, stride=4), :]
                new_pot[rows, :] = pot[rows, :] + STEP * (target[rows, :] - mass)

        some = pl.ds(q * size, size)
        sends.append(pltpu.make_async_copy(moments.at[some], moments_hbm.at[some], sems.at[q]))
        sends[-1].start()
    sends.append(pltpu.make_async_copy(new_pot, new_pot_hbm, sems.at[parts]))
    sends[-1].start()
    row = lax.broadcasted_iota(jnp.int32, (ROWS, BS), 0).astype(jnp.float32)
    total = None
    for half in range(2):
        fill = None
        for j in range(4):
            index = got[4 * half + j, PAIR_CAP : PAIR_CAP + 1, :]
            fill = index if fill is None else jnp.maximum(fill, index)
        hot = bf(jnp.where(row == fill, 1.0, 0.0))
        rest = jnp.concatenate([got[4 * half + j, :PAIR_CAP, :] for j in range(4)], axis=0)
        for _ in range(3):
            piece = bf(rest)
            rest = rest - f32(piece)
            term = jnp.dot(hot, piece, preferred_element_type=jnp.float32)
            total = term if total is None else total + term
    dual_pot[...] = total
    sends.append(pltpu.make_async_copy(dual_pot, dual_hbm, sems.at[parts + 1]))
    sends[-1].start()
    for send in sends:
        send.wait()


def total(own, above_in, below_in, got, pot, target):
    shapes = [(ROWS, BS), (4 * SB, BS), (SB, BS)]
    return pl.pallas_call(
        total_kernel,
        in_specs=[VMEM] * 6,
        out_specs=[HBM] * 3,
        out_shape=[jax.ShapeDtypeStruct(shape, jnp.float32) for shape in shapes],
        scratch_shapes=[
            pltpu.VMEM((4 * SB, BS), jnp.float32),
            pltpu.VMEM((SB, BS), jnp.float32),
            pltpu.VMEM((ROWS, BS), jnp.float32),
            pltpu.SemaphoreType.DMA((6,)),
        ],
        compiler_params=pltpu.CompilerParams(vmem_limit_bytes=16 << 20),
        name="total",
    )(own, above_in, below_in, got, pot, target)


BUFFERS = ("split", "xat", "part", "top", "f8")


def work_kernel(
    pidx, plan, vox_hbm, mass_hbm, ypool,
    low_out, own_out, high_out, dual, mom, vox, mass, sems, order, place, ranks, *scratch,
):
    loads = [
        pltpu.make_async_copy(vox_hbm, vox, sems.at[0]),
        pltpu.make_async_copy(mass_hbm, mass, sems.at[1]),
    ]
    for load in loads:
        load.start()
    first_lane = (lax.axis_index("gy") & 3) * PAIR_CAP
    for g in range(N_GY):
        ranks[g] = 0

    def compact(h, n):
        for u in range(2):
            v = 2 * h + u
            p = plan[v]
            occupied = (p >= 0).astype(jnp.int32)
            dest = (p >> 7) & 7
            rank = ranks[dest]
            ranks[dest] = rank + occupied
            order[n] = v
            place[n] = (dest << 16) | (rank << 8) | (p & 127)
            n = n + occupied
            for j in range(POOL // VB):
                mom[v * (POOL // VB) + j] = jnp.zeros((8, BS), jnp.float32)
        return n

    n = lax.fori_loop(0, VB // 2, compact, jnp.int32(0))
    for load in loads:
        load.wait()
    size = len(BUFFERS)
    bufs = [dict(zip(BUFFERS, scratch[i * size : (i + 1) * size])) for i in range(SLOTS * TOGETHER)]
    lane = lax.broadcasted_iota(jnp.int32, (1, BS), 1)
    dual[...] = jnp.full(dual.shape, -1.0, jnp.float32)

    def prepare(t, b):
        s = order[t]
        x = vox[pl.ds(s, 3, stride=VB), :] - 0.5
        xh = f32(bf(x))
        xl = x - xh
        tops = [f32(ypool[pidx[s * KC + k], 0:8, :]) for k in range(KC)]
        while len(tops) > 1:
            tops = [jnp.maximum(a, c) for a, c in zip(tops[::2], tops[1::2])]
        top = jnp.max(tops[0][3:4], axis=1, keepdims=True)
        top = jnp.broadcast_to(top, (1, BS))
        one = jnp.ones((1, BS), jnp.float32)
        xa = jnp.concatenate([xh, one, xh, one, xl, one, xl, -top], axis=0)
        b["xat"][...] = bf(xa.T)
        b["top"][0:1, :] = top

    def weigh_and_spread(t, b, told, bold):
        part = None
        s = order[t] if t is not None else None
        sold = order[told] if told is not None else None
        for c in range(KC // 2):
            if t is not None:
                y = [ypool[pidx[s * KC + 2 * c + j]] for j in range(2)]
                sc = jnp.dot(
                    b["xat"][...],
                    jnp.concatenate(y, axis=1),
                    preferred_element_type=jnp.float32,
                )
            if told is not None:
                e2 = jnp.concatenate([bold["split"][2 * c], bold["split"][2 * c + 1]], axis=1)
                m = jnp.dot(bold["f8"][...], e2, preferred_element_type=jnp.float32)
                for j in range(2):
                    mom[pidx[sold * KC + 2 * c + j]] += m[:, j * BS : (j + 1) * BS]
            if t is not None:
                e = jnp.exp2(sc)
                eh = bf(e)
                el = bf(e - f32(eh))
                for j in range(2):
                    b["split"][2 * c + j, 0:BS, :] = eh[:, j * BS : (j + 1) * BS]
                    b["split"][2 * c + j, BS:, :] = el[:, j * BS : (j + 1) * BS]
                p = e[:, :BS] + e[:, BS:]
                part = p if part is None else part + p
        if t is not None:
            b["part"][...] = part

    def norm(t, b):
        s = order[t]
        d = jnp.sum(b["part"][...].T, axis=0, keepdims=True)
        xr = vox[pl.ds(s, 3, stride=VB), :]
        x = xr - 0.5
        sq = jnp.sum(x * x, axis=0, keepdims=True)
        where = place[t]
        top_row = (where >> 16) * GROUP
        rank = (where >> 8) & 255
        mark = pl.ds(top_row + PAIR_CAP, 1)
        dual[mark, :] = jnp.where(
            lane == first_lane + rank, (where & 255).astype(jnp.float32), dual[mark, :]
        )
        dual[pl.ds(top_row + rank, 1), :] = (1.0 / EPS) * sq - LN2 * (b["top"][0:1, :] + jnp.log2(d))
        w = mass[pl.ds(s, 1), :] / d
        f = jnp.concatenate([w, xr * w], axis=0)
        fh = f32(bf(f))
        f8 = bf(jnp.concatenate([fh, f - fh], axis=0))
        b["f8"][...] = jnp.concatenate([f8, f8], axis=1)

    def step(g, slot, valid):
        for stage in range(3):
            for u in range(TOGETHER):
                at = lambda lag: (g - lag) * TOGETHER + u if valid(lag) else None
                buf = lambda lag: bufs[((slot - lag) % SLOTS) * TOGETHER + u]
                if stage == 0 and valid(0):
                    prepare(at(0), buf(0))
                if stage == 1 and (valid(1) or valid(3)):
                    weigh_and_spread(at(1), buf(1), at(3), buf(3))
                if stage == 2 and valid(2):
                    norm(at(2), buf(2))

    groups = n // TOGETHER

    @pl.when(n > 0)
    def _():
        for g in range(SLOTS):
            step(g, g, lambda lag: lag <= g)

        @pl.loop(0, (groups - SLOTS) // SLOTS)
        def _(h):
            for u in range(SLOTS):
                step(SLOTS + SLOTS * h + u, u, lambda lag: True)

        for e in range(3):
            step(groups + e, e, lambda lag: lag > e)

    for q, out in enumerate((low_out, own_out, high_out)):

        @pl.loop(0, SB // 16)
        def _(g):
            for j in range(16):
                m = mom[q * SB + g * 16 + j]
                out[g * 16 + j] = m[0:4] + m[4:8]


def work(pidx, plan, vox, mass, ypool):
    moments = jax.ShapeDtypeStruct((SB, 4, BS), jnp.float32)
    scratch = [
        pltpu.VMEM((POOL, 8, BS), jnp.float32),
        pltpu.VMEM((3 * VB, BS), jnp.float32),
        pltpu.VMEM((VB, BS), jnp.float32),
        pltpu.SemaphoreType.DMA((2,)),
        pltpu.SMEM((VB + 8,), jnp.int32),
        pltpu.SMEM((VB + 8,), jnp.int32),
        pltpu.SMEM((N_GY,), jnp.int32),
    ]
    scratch += [
        pltpu.VMEM((KC, 2 * BS, BS), jnp.bfloat16),
        pltpu.VMEM((BS, 16), jnp.bfloat16),
        pltpu.VMEM((BS, BS), jnp.float32),
        pltpu.VMEM((8, BS), jnp.float32),
        pltpu.VMEM((8, 2 * BS), jnp.bfloat16),
    ] * (SLOTS * TOGETHER)
    return pl.pallas_call(
        work_kernel,
        in_specs=[SMEM] * 2 + [HBM] * 2 + [VMEM],
        out_specs=[VMEM] * 4,
        out_shape=[moments] * 3 + [jax.ShapeDtypeStruct((N_GY * GROUP, BS), jnp.float32)],
        scratch_shapes=scratch,
        compiler_params=pltpu.CompilerParams(vmem_limit_bytes=32 << 20),
        name="work",
    )(
        pidx,
        plan,
        pltpu.with_memory_space_constraint(vox, pltpu.HBM),
        pltpu.with_memory_space_constraint(mass, pltpu.HBM),
        ypool,
    )


def on_device(
    voxel_xyz, voxel_mass, candidates, offload_plan, seed_xyz, seed_pot, seed_target, seed_home
):
    ypool, pidx = exchange(
        jnp.transpose(seed_xyz, (1, 0, 2)), seed_pot, candidates.T, seed_home
    )
    vox = jnp.transpose(voxel_xyz, (1, 0, 2)).reshape(3 * VB, BS)
    low, own, high, dual = work(pidx, offload_plan, vox, voxel_mass, ypool)
    flat = lambda m: m.reshape(4 * SB, BS)
    above_in, below_in, got = deliver(flat(low), flat(high), dual.reshape(N_GY, GROUP, BS))
    dual_pot, moments, new_pot = total(
        flat(own), above_in, below_in, got, seed_pot, seed_target
    )
    return (dual_pot, moments.reshape(SB, 4, BS), new_pot)


def solution(mesh):
    return jax.shard_map(
        on_device,
        mesh=mesh,
        in_specs=(
            P(("gx", "gy"), None, None),
            P(("gx", "gy"), None),
            P(("gx", "gy"), None),
            P(("gx", "gy")),
            P(("gx", "gy"), None, None),
            P(("gx", "gy"), None),
            P(("gx", "gy"), None),
            P(),
        ),
        out_specs=(P(("gx", "gy"), None), P(("gx", "gy"), None, None), P(("gx", "gy"), None)),
        check_vma=False,
    )
```

```python
import math

import jax
import jax.numpy as jnp
from jax import lax
from jax.experimental import pallas as pl
from jax.experimental.pallas import tpu as pltpu
from jax.sharding import PartitionSpec as P

BS = 128
KC = 8
PAIR_CAP = 32
VB = 256
SB = 512
POOL = 3 * SB
N_GX = 16
N_GY = 8
ROWS = 128
GROUP = 40
SLOTS = 4
TOGETHER = 4
CHUNKS = 4

EPS = 0.05
STEP = 0.5
LOG2E = math.log2(math.e)
LN2 = math.log(2.0)

VMEM = pl.BlockSpec(memory_space=pltpu.VMEM)
SMEM = pl.BlockSpec(memory_space=pltpu.SMEM)
HBM = pl.BlockSpec(memory_space=pltpu.HBM)
MESH = pl.DeviceIdType.MESH


def bf(x):
    return x.astype(jnp.bfloat16)


def f32(x):
    return x.astype(jnp.float32)


def meet(peers):
    barrier = pltpu.get_barrier_semaphore()
    for peer in peers:
        pl.semaphore_signal(barrier, inc=1, device_id=peer, device_id_type=MESH)
    pl.semaphore_wait(barrier, len(peers))


def exchange_kernel(
    xyz_hbm, pot_hbm, cand_hbm, home_hbm, ypool, pidx,
    xyz, pot, plane, cand, home, load_sem, send_sem, recv_sem,
):
    x, g = lax.axis_index("gx"), lax.axis_index("gy")
    below, above = (x + N_GX - 1) % N_GX, (x + 1) % N_GX
    pairs = (
        (xyz_hbm, xyz.at[1]), (pot_hbm, pot.at[1]), (cand_hbm, cand), (home_hbm, home)
    )
    loads = [pltpu.make_async_copy(a, b, load_sem.at[i]) for i, (a, b) in enumerate(pairs)]
    for load in loads:
        load.start()
    meet([(below, g), (above, g)])
    copies = []
    for q in range(CHUNKS):
        some = pl.ds(q * (SB // CHUNKS), SB // CHUNKS)
        for way, (slot, peer) in enumerate(((0, above), (2, below))):
            for kind, (source, dest) in enumerate(
                (
                    (xyz_hbm.at[:, some, :], xyz.at[slot, :, some, :]),
                    (pot_hbm.at[some, :], pot.at[slot, some, :]),
                )
            ):
                i = (q * 2 + way) * 2 + kind
                copy = pltpu.make_async_remote_copy(
                    source, dest, send_sem.at[i], recv_sem.at[i],
                    device_id=(peer, g), device_id_type=MESH,
                )
                copy.start()
                copies.append(copy)

    sub = lax.broadcasted_iota(jnp.int32, (8, BS), 0)
    low = sub < 4

    def build(slot, start, count):
        @pl.loop(0, count // 16)
        def _(i):
            at = pl.multiple_of(start + i * 16, 16)
            square = None
            for c in range(3):
                y = xyz[slot, c, pl.ds(at, 16), :] - 0.5
                plane[c * 16 : (c + 1) * 16, :] = (2.0 * LOG2E / EPS) * y
                square = y * y if square is None else square + y * y
            plane[48:64, :] = LOG2E * (pot[slot, pl.ds(at, 16), :] - (1.0 / EPS) * square)
            for j in range(16):
                t = plane[pl.ds(j, 4, stride=16), :]
                a = jnp.concatenate([t, t], axis=0)
                hi = f32(bf(a))
                mid = f32(bf(a - hi))
                first = jnp.where(low, hi, mid)
                second = jnp.where(sub == 3, a - hi - mid, jnp.where(sub == 7, 1.0, first))
                ypool[slot * SB + at + j] = bf(jnp.concatenate([first, second], axis=0))

    loads[0].wait()
    loads[1].wait()
    build(1, 0, SB)
    loads[2].wait()
    loads[3].wait()

    @pl.loop(0, VB // 2)
    def _(h):
        for u in range(2):
            v = 2 * h + u
            for k in range(KC):
                s = home[cand[k, v]]
                pidx[v * KC + k] = ((((s >> 12) - x + 1) & 15) << 9) | (s & 511)

    for q in range(CHUNKS):
        for copy in copies[4 * q : 4 * q + 4]:
            copy.wait_recv()
        for slot in (0, 2):
            build(slot, q * (SB // CHUNKS), SB // CHUNKS)
    for copy in copies:
        copy.wait_send()


def exchange(xyz, pot, cand, home):
    return pl.pallas_call(
        exchange_kernel,
        in_specs=[HBM] * 4,
        out_specs=[VMEM, SMEM],
        out_shape=[
            jax.ShapeDtypeStruct((POOL, 16, BS), jnp.bfloat16),
            jax.ShapeDtypeStruct((VB * KC,), jnp.int32),
        ],
        scratch_shapes=[
            pltpu.VMEM((3, 3, SB, BS), jnp.float32),
            pltpu.VMEM((3, SB, BS), jnp.float32),
            pltpu.VMEM((64, BS), jnp.float32),
            pltpu.SMEM((KC, VB), jnp.int32),
            pltpu.SMEM((N_GX * N_GY * SB,), jnp.int32),
            pltpu.SemaphoreType.DMA((4,)),
            pltpu.SemaphoreType.DMA((4 * CHUNKS,)),
            pltpu.SemaphoreType.DMA((4 * CHUNKS,)),
        ],
        compiler_params=pltpu.CompilerParams(
            collective_id=0, has_side_effects=True, vmem_limit_bytes=16 << 20
        ),
        name="exchange",
    )(*(pltpu.with_memory_space_constraint(a, pltpu.HBM) for a in (xyz, pot, cand, home)))


def deliver_kernel(
    low, high, dual, above_in, below_in, got, dual_send, dual_recv, send_sem, recv_sem, own_sem
):
    x, g = lax.axis_index("gx"), lax.axis_index("gy")
    below, above = (x + N_GX - 1) % N_GX, (x + 1) % N_GX
    others = [(g + d) % N_GY for d in range(1, N_GY)]
    meet([(below, g), (above, g)] + [(x, peer) for peer in others])
    copies = [
        pltpu.make_async_remote_copy(
            low, above_in, send_sem.at[0], recv_sem.at[0],
            device_id=(below, g), device_id_type=MESH,
        ),
        pltpu.make_async_remote_copy(
            high, below_in, send_sem.at[1], recv_sem.at[1],
            device_id=(above, g), device_id_type=MESH,
        ),
    ]
    for d, peer in enumerate(others):
        copies.append(
            pltpu.make_async_remote_copy(
                dual.at[peer], got.at[g], dual_send.at[d], dual_recv.at[d],
                device_id=(x, peer), device_id_type=MESH,
            )
        )
    keep = pltpu.make_async_copy(dual.at[g], got.at[g], own_sem)
    for copy in copies:
        copy.start()
    keep.start()
    keep.wait()
    for copy in copies:
        copy.wait()


def deliver(low, high, dual):
    moments = jax.ShapeDtypeStruct((4 * SB, BS), jnp.float32)
    return pl.pallas_call(
        deliver_kernel,
        in_specs=[VMEM] * 3,
        out_specs=[VMEM] * 3,
        out_shape=[moments] * 2 + [jax.ShapeDtypeStruct((N_GY, GROUP, BS), jnp.float32)],
        scratch_shapes=[
            pltpu.SemaphoreType.DMA((N_GY - 1,)),
            pltpu.SemaphoreType.DMA((N_GY - 1,)),
            pltpu.SemaphoreType.DMA((2,)),
            pltpu.SemaphoreType.DMA((2,)),
            pltpu.SemaphoreType.DMA(()),
        ],
        compiler_params=pltpu.CompilerParams(
            collective_id=1, has_side_effects=True, vmem_limit_bytes=16 << 20
        ),
        name="deliver",
    )(low, high, dual)


def total_kernel(
    own, above_in, below_in, got, pot, target, dual_hbm, moments_hbm, new_pot_hbm,
    moments, new_pot, dual_pot, sems,
):
    parts = 4
    size = 4 * SB // parts
    sends = []
    for q in range(parts):

        @pl.loop(0, SB // 16 // parts)
        def _(i):
            at = pl.multiple_of(q * size + i * 64, 64)
            moments[pl.ds(at, 64), :] = (
                own[pl.ds(at, 64), :] + above_in[pl.ds(at, 64), :] + below_in[pl.ds(at, 64), :]
            )
            for j in range(2):
                rows = pl.ds(pl.multiple_of(q * (size // 4) + i * 16, 16) + 8 * j, 8)
                mass = moments[pl.ds(at + 32 * j, 8, stride=4), :]
                new_pot[rows, :] = pot[rows, :] + STEP * (target[rows, :] - mass)

        some = pl.ds(q * size, size)
        sends.append(pltpu.make_async_copy(moments.at[some], moments_hbm.at[some], sems.at[q]))
        sends[-1].start()
    sends.append(pltpu.make_async_copy(new_pot, new_pot_hbm, sems.at[parts]))
    sends[-1].start()
    row = lax.broadcasted_iota(jnp.int32, (ROWS, BS), 0).astype(jnp.float32)
    total = None
    for half in range(2):
        fill = None
        for j in range(4):
            index = got[4 * half + j, PAIR_CAP : PAIR_CAP + 1, :]
            fill = index if fill is None else jnp.maximum(fill, index)
        hot = bf(jnp.where(row == fill, 1.0, 0.0))
        rest = jnp.concatenate([got[4 * half + j, :PAIR_CAP, :] for j in range(4)], axis=0)
        for _ in range(3):
            piece = bf(rest)
            rest = rest - f32(piece)
            term = jnp.dot(hot, piece, preferred_element_type=jnp.float32)
            total = term if total is None else total + term
    dual_pot[...] = total
    sends.append(pltpu.make_async_copy(dual_pot, dual_hbm, sems.at[parts + 1]))
    sends[-1].start()
    for send in sends:
        send.wait()


def total(own, above_in, below_in, got, pot, target):
    shapes = [(ROWS, BS), (4 * SB, BS), (SB, BS)]
    return pl.pallas_call(
        total_kernel,
        in_specs=[VMEM] * 6,
        out_specs=[HBM] * 3,
        out_shape=[jax.ShapeDtypeStruct(shape, jnp.float32) for shape in shapes],
        scratch_shapes=[
            pltpu.VMEM((4 * SB, BS), jnp.float32),
            pltpu.VMEM((SB, BS), jnp.float32),
            pltpu.VMEM((ROWS, BS), jnp.float32),
            pltpu.SemaphoreType.DMA((6,)),
        ],
        compiler_params=pltpu.CompilerParams(vmem_limit_bytes=16 << 20),
        name="total",
    )(own, above_in, below_in, got, pot, target)


BUFFERS = ("split", "xat", "part", "top", "f8")


def work_kernel(
    pidx, plan, vox_hbm, mass_hbm, ypool,
    low_out, own_out, high_out, dual, mom, vox, mass, sems, order, place, ranks, *scratch,
):
    loads = [
        pltpu.make_async_copy(vox_hbm, vox, sems.at[0]),
        pltpu.make_async_copy(mass_hbm, mass, sems.at[1]),
    ]
    for load in loads:
        load.start()
    first_lane = (lax.axis_index("gy") & 3) * PAIR_CAP
    for g in range(N_GY):
        ranks[g] = 0

    def compact(h, n):
        for u in range(2):
            v = 2 * h + u
            p = plan[v]
            occupied = (p >= 0).astype(jnp.int32)
            dest = (p >> 7) & 7
            rank = ranks[dest]
            ranks[dest] = rank + occupied
            order[n] = v
            place[n] = (dest << 16) | (rank << 8) | (p & 127)
            n = n + occupied
            for j in range(POOL // VB):
                mom[v * (POOL // VB) + j] = jnp.zeros((8, BS), jnp.float32)
        return n

    n = lax.fori_loop(0, VB // 2, compact, jnp.int32(0))
    for load in loads:
        load.wait()
    size = len(BUFFERS)
    bufs = [dict(zip(BUFFERS, scratch[i * size : (i + 1) * size])) for i in range(SLOTS * TOGETHER)]
    lane = lax.broadcasted_iota(jnp.int32, (1, BS), 1)
    dual[...] = jnp.full(dual.shape, -1.0, jnp.float32)

    def prepare(t, b):
        s = order[t]
        x = vox[pl.ds(s, 3, stride=VB), :] - 0.5
        xh = f32(bf(x))
        xl = x - xh
        tops = [f32(ypool[pidx[s * KC + k], 0:8, :]) for k in range(KC)]
        while len(tops) > 1:
            tops = [jnp.maximum(a, c) for a, c in zip(tops[::2], tops[1::2])]
        top = jnp.max(tops[0][3:4], axis=1, keepdims=True)
        top = jnp.broadcast_to(top, (1, BS))
        one = jnp.ones((1, BS), jnp.float32)
        xa = jnp.concatenate([xh, one, xh, one, xl, one, xl, -top], axis=0)
        b["xat"][...] = bf(xa.T)
        b["top"][0:1, :] = top

    def score(t, b, c):
        s = order[t]
        y = [ypool[pidx[s * KC + 2 * c + j]] for j in range(2)]
        return jnp.dot(
            b["xat"][...], jnp.concatenate(y, axis=1), preferred_element_type=jnp.float32
        )

    def spread(t, b, c):
        s = order[t]
        e = jnp.concatenate([b["split"][2 * c], b["split"][2 * c + 1]], axis=1)
        m = jnp.dot(b["f8"][...], e, preferred_element_type=jnp.float32)
        for j in range(2):
            mom[pidx[s * KC + 2 * c + j]] += m[:, j * BS : (j + 1) * BS]

    def weigh(sc, b, c, part):
        e = jnp.exp2(sc)
        eh = bf(e)
        el = bf(e - f32(eh))
        for j in range(2):
            b["split"][2 * c + j, 0:BS, :] = eh[:, j * BS : (j + 1) * BS]
            b["split"][2 * c + j, BS:, :] = el[:, j * BS : (j + 1) * BS]
        p = e[:, :BS] + e[:, BS:]
        return p if part is None else part + p

    def weigh_and_spread(new, old):
        parts = [None] * len(new)
        for c in range(KC // 2):
            scores = [score(t, b, c) for t, b in new]
            for t, b in old:
                spread(t, b, c)
            parts = [weigh(sc, b, c, p) for sc, (t, b), p in zip(scores, new, parts)]
        for p, (t, b) in zip(parts, new):
            b["part"][...] = p

    def norm(t, b):
        s = order[t]
        d = jnp.sum(b["part"][...].T, axis=0, keepdims=True)
        xr = vox[pl.ds(s, 3, stride=VB), :]
        x = xr - 0.5
        sq = jnp.sum(x * x, axis=0, keepdims=True)
        where = place[t]
        top_row = (where >> 16) * GROUP
        rank = (where >> 8) & 255
        mark = pl.ds(top_row + PAIR_CAP, 1)
        dual[mark, :] = jnp.where(
            lane == first_lane + rank, (where & 255).astype(jnp.float32), dual[mark, :]
        )
        dual[pl.ds(top_row + rank, 1), :] = (1.0 / EPS) * sq - LN2 * (b["top"][0:1, :] + jnp.log2(d))
        w = mass[pl.ds(s, 1), :] / d
        f = jnp.concatenate([w, xr * w], axis=0)
        fh = f32(bf(f))
        f8 = bf(jnp.concatenate([fh, f - fh], axis=0))
        b["f8"][...] = jnp.concatenate([f8, f8], axis=1)

    def step(g, slot, valid):
        def blocks(lag):
            if not valid(lag):
                return []
            first = ((slot - lag) % SLOTS) * TOGETHER
            return [((g - lag) * TOGETHER + u, bufs[first + u]) for u in range(TOGETHER)]

        for t, b in blocks(0):
            prepare(t, b)
        new, old = blocks(1), blocks(3)
        for u in range(0, TOGETHER, 2):
            weigh_and_spread(new[u : u + 2], old[u : u + 2])
        for t, b in blocks(2):
            norm(t, b)

    groups = n // TOGETHER

    @pl.when(n > 0)
    def _():
        for g in range(SLOTS):
            step(g, g, lambda lag: lag <= g)

        @pl.loop(0, (groups - SLOTS) // SLOTS)
        def _(h):
            for u in range(SLOTS):
                step(SLOTS + SLOTS * h + u, u, lambda lag: True)

        for e in range(3):
            step(groups + e, e, lambda lag: lag > e)

    for q, out in enumerate((low_out, own_out, high_out)):

        @pl.loop(0, SB // 16)
        def _(g):
            for j in range(16):
                m = mom[q * SB + g * 16 + j]
                out[g * 16 + j] = m[0:4] + m[4:8]


def work(pidx, plan, vox, mass, ypool):
    moments = jax.ShapeDtypeStruct((SB, 4, BS), jnp.float32)
    scratch = [
        pltpu.VMEM((POOL, 8, BS), jnp.float32),
        pltpu.VMEM((3 * VB, BS), jnp.float32),
        pltpu.VMEM((VB, BS), jnp.float32),
        pltpu.SemaphoreType.DMA((2,)),
        pltpu.SMEM((VB + 8,), jnp.int32),
        pltpu.SMEM((VB + 8,), jnp.int32),
        pltpu.SMEM((N_GY,), jnp.int32),
    ]
    scratch += [
        pltpu.VMEM((KC, 2 * BS, BS), jnp.bfloat16),
        pltpu.VMEM((BS, 16), jnp.bfloat16),
        pltpu.VMEM((BS, BS), jnp.float32),
        pltpu.VMEM((8, BS), jnp.float32),
        pltpu.VMEM((8, 2 * BS), jnp.bfloat16),
    ] * (SLOTS * TOGETHER)
    return pl.pallas_call(
        work_kernel,
        in_specs=[SMEM] * 2 + [HBM] * 2 + [VMEM],
        out_specs=[VMEM] * 4,
        out_shape=[moments] * 3 + [jax.ShapeDtypeStruct((N_GY * GROUP, BS), jnp.float32)],
        scratch_shapes=scratch,
        compiler_params=pltpu.CompilerParams(vmem_limit_bytes=32 << 20),
        name="work",
    )(
        pidx,
        plan,
        pltpu.with_memory_space_constraint(vox, pltpu.HBM),
        pltpu.with_memory_space_constraint(mass, pltpu.HBM),
        ypool,
    )


def on_device(
    voxel_xyz, voxel_mass, candidates, offload_plan, seed_xyz, seed_pot, seed_target, seed_home
):
    ypool, pidx = exchange(
        jnp.transpose(seed_xyz, (1, 0, 2)), seed_pot, candidates.T, seed_home
    )
    vox = jnp.transpose(voxel_xyz, (1, 0, 2)).reshape(3 * VB, BS)
    low, own, high, dual = work(pidx, offload_plan, vox, voxel_mass, ypool)
    flat = lambda m: m.reshape(4 * SB, BS)
    above_in, below_in, got = deliver(flat(low), flat(high), dual.reshape(N_GY, GROUP, BS))
    dual_pot, moments, new_pot = total(
        flat(own), above_in, below_in, got, seed_pot, seed_target
    )
    return (dual_pot, moments.reshape(SB, 4, BS), new_pot)


def solution(mesh):
    return jax.shard_map(
        on_device,
        mesh=mesh,
        in_specs=(
            P(("gx", "gy"), None, None),
            P(("gx", "gy"), None),
            P(("gx", "gy"), None),
            P(("gx", "gy")),
            P(("gx", "gy"), None, None),
            P(("gx", "gy"), None),
            P(("gx", "gy"), None),
            P(),
        ),
        out_specs=(P(("gx", "gy"), None), P(("gx", "gy"), None, None), P(("gx", "gy"), None)),
        check_vma=False,
    )
```

```python
import math

import jax
import jax.numpy as jnp
from jax import lax
from jax.experimental import pallas as pl
from jax.experimental.pallas import tpu as pltpu
from jax.sharding import PartitionSpec as P

BS = 128
KC = 8
PAIR_CAP = 32
VB = 256
SB = 512
POOL = 3 * SB
N_GX = 16
N_GY = 8
ROWS = 128
GROUP = 40
SLOTS = 4
TOGETHER = 4
CHUNKS = 4

EPS = 0.05
STEP = 0.5
LOG2E = math.log2(math.e)
LN2 = math.log(2.0)

VMEM = pl.BlockSpec(memory_space=pltpu.VMEM)
SMEM = pl.BlockSpec(memory_space=pltpu.SMEM)
HBM = pl.BlockSpec(memory_space=pltpu.HBM)
MESH = pl.DeviceIdType.MESH


def bf(x):
    return x.astype(jnp.bfloat16)


def f32(x):
    return x.astype(jnp.float32)


def meet(peers):
    barrier = pltpu.get_barrier_semaphore()
    for peer in peers:
        pl.semaphore_signal(barrier, inc=1, device_id=peer, device_id_type=MESH)
    pl.semaphore_wait(barrier, len(peers))


def exchange_kernel(
    xyz_hbm, pot_hbm, cand_hbm, home_hbm, plan_hbm, ypool, pidx, listed,
    xyz, pot, plane, cand, home, plan, load_sem, send_sem, recv_sem,
):
    x, g = lax.axis_index("gx"), lax.axis_index("gy")
    below, above = (x + N_GX - 1) % N_GX, (x + 1) % N_GX
    pairs = (
        (xyz_hbm, xyz.at[1]), (pot_hbm, pot.at[1]), (cand_hbm, cand), (home_hbm, home),
        (plan_hbm, plan),
    )
    loads = [pltpu.make_async_copy(a, b, load_sem.at[i]) for i, (a, b) in enumerate(pairs)]
    for load in loads:
        load.start()
    meet([(below, g), (above, g)])
    copies = []
    for q in range(CHUNKS):
        some = pl.ds(q * (SB // CHUNKS), SB // CHUNKS)
        for way, (slot, peer) in enumerate(((0, above), (2, below))):
            for kind, (source, dest) in enumerate(
                (
                    (xyz_hbm.at[:, some, :], xyz.at[slot, :, some, :]),
                    (pot_hbm.at[some, :], pot.at[slot, some, :]),
                )
            ):
                i = (q * 2 + way) * 2 + kind
                copy = pltpu.make_async_remote_copy(
                    source, dest, send_sem.at[i], recv_sem.at[i],
                    device_id=(peer, g), device_id_type=MESH,
                )
                copy.start()
                copies.append(copy)

    sub = lax.broadcasted_iota(jnp.int32, (8, BS), 0)
    low = sub < 4

    def build(slot, start, count):
        @pl.loop(0, count // 16)
        def _(i):
            at = pl.multiple_of(start + i * 16, 16)
            square = None
            for c in range(3):
                y = xyz[slot, c, pl.ds(at, 16), :] - 0.5
                plane[c * 16 : (c + 1) * 16, :] = (2.0 * LOG2E / EPS) * y
                square = y * y if square is None else square + y * y
            plane[48:64, :] = LOG2E * (pot[slot, pl.ds(at, 16), :] - (1.0 / EPS) * square)
            for j in range(16):
                t = plane[pl.ds(j, 4, stride=16), :]
                a = jnp.concatenate([t, t], axis=0)
                hi = f32(bf(a))
                mid = f32(bf(a - hi))
                first = jnp.where(low, hi, mid)
                second = jnp.where(sub == 3, a - hi - mid, jnp.where(sub == 7, 1.0, first))
                ypool[slot * SB + at + j] = bf(jnp.concatenate([first, second], axis=0))

    loads[0].wait()
    loads[1].wait()
    build(1, 0, SB)
    loads[4].wait()
    p = jnp.concatenate([plan[0:1, :], plan[1:2, :]], axis=1)
    wide = lambda axis, rows: lax.broadcasted_iota(jnp.int32, (rows, VB), axis)
    taken = jnp.broadcast_to(p >= 0, (8, VB))
    dest = jnp.broadcast_to((p >> 7) & 7, (8, VB))
    one_hot = jnp.where(taken, jnp.where(dest == wide(0, 8), 1.0, 0.0), 0.0)
    before = jnp.where(wide(0, VB) < wide(1, VB), 1.0, 0.0)
    earlier = jnp.dot(bf(one_hot), bf(before), preferred_element_type=jnp.float32)
    rank = jnp.sum(earlier * one_hot, axis=0, keepdims=True)
    place = jnp.sum(earlier, axis=0, keepdims=True)
    place = jnp.where(p >= 0, place, -1.0)
    chosen = jnp.where(place == wide(0, VB).astype(jnp.float32), 1.0, 0.0)
    facts = [
        wide(1, 1).astype(jnp.float32),
        ((p >> 7) & 7).astype(jnp.float32),
        rank,
        (p & 127).astype(jnp.float32),
        jnp.zeros((4, VB), jnp.float32),
    ]
    facts = lax.dot_general(
        bf(jnp.concatenate(facts, axis=0)),
        bf(chosen),
        (((1,), (1,)), ((), ())),
        preferred_element_type=jnp.float32,
    ).astype(jnp.int32)
    count = jnp.sum(one_hot, axis=(0, 1), keepdims=True).astype(jnp.int32)
    listed[0:1, :] = facts[0:1]
    listed[1:2, :] = (facts[1:2] << 16) | (facts[2:3] << 8) | facts[3:4]
    listed[2:8, :] = jnp.broadcast_to(count, (6, VB))
    loads[2].wait()
    loads[3].wait()

    @pl.loop(0, VB // 2)
    def _(h):
        for u in range(2):
            v = 2 * h + u
            for k in range(KC):
                s = home[cand[k, v]]
                pidx[v * KC + k] = ((((s >> 12) - x + 1) & 15) << 9) | (s & 511)

    for q in range(CHUNKS):
        for copy in copies[4 * q : 4 * q + 4]:
            copy.wait_recv()
        for slot in (0, 2):
            build(slot, q * (SB // CHUNKS), SB // CHUNKS)
    for copy in copies:
        copy.wait_send()


def exchange(xyz, pot, cand, home, plan):
    return pl.pallas_call(
        exchange_kernel,
        in_specs=[HBM] * 5,
        out_specs=[VMEM, SMEM, VMEM],
        out_shape=[
            jax.ShapeDtypeStruct((POOL, 16, BS), jnp.bfloat16),
            jax.ShapeDtypeStruct((VB * KC,), jnp.int32),
            jax.ShapeDtypeStruct((8, VB), jnp.int32),
        ],
        scratch_shapes=[
            pltpu.VMEM((3, 3, SB, BS), jnp.float32),
            pltpu.VMEM((3, SB, BS), jnp.float32),
            pltpu.VMEM((64, BS), jnp.float32),
            pltpu.SMEM((KC, VB), jnp.int32),
            pltpu.SMEM((N_GX * N_GY * SB,), jnp.int32),
            pltpu.VMEM((VB // BS, BS), jnp.int32),
            pltpu.SemaphoreType.DMA((5,)),
            pltpu.SemaphoreType.DMA((4 * CHUNKS,)),
            pltpu.SemaphoreType.DMA((4 * CHUNKS,)),
        ],
        compiler_params=pltpu.CompilerParams(
            collective_id=0, has_side_effects=True, vmem_limit_bytes=16 << 20
        ),
        name="exchange",
    )(*(pltpu.with_memory_space_constraint(a, pltpu.HBM) for a in (xyz, pot, cand, home, plan)))


def deliver_kernel(
    low, high, dual, above_in, below_in, got, dual_send, dual_recv, send_sem, recv_sem, own_sem
):
    x, g = lax.axis_index("gx"), lax.axis_index("gy")
    below, above = (x + N_GX - 1) % N_GX, (x + 1) % N_GX
    others = [(g + d) % N_GY for d in range(1, N_GY)]
    meet([(below, g), (above, g)] + [(x, peer) for peer in others])
    copies = [
        pltpu.make_async_remote_copy(
            low, above_in, send_sem.at[0], recv_sem.at[0],
            device_id=(below, g), device_id_type=MESH,
        ),
        pltpu.make_async_remote_copy(
            high, below_in, send_sem.at[1], recv_sem.at[1],
            device_id=(above, g), device_id_type=MESH,
        ),
    ]
    for d, peer in enumerate(others):
        copies.append(
            pltpu.make_async_remote_copy(
                dual.at[peer], got.at[g], dual_send.at[d], dual_recv.at[d],
                device_id=(x, peer), device_id_type=MESH,
            )
        )
    keep = pltpu.make_async_copy(dual.at[g], got.at[g], own_sem)
    for copy in copies:
        copy.start()
    keep.start()
    keep.wait()
    for copy in copies:
        copy.wait()


def deliver(low, high, dual):
    moments = jax.ShapeDtypeStruct((4 * SB, BS), jnp.float32)
    return pl.pallas_call(
        deliver_kernel,
        in_specs=[VMEM] * 3,
        out_specs=[VMEM] * 3,
        out_shape=[moments] * 2 + [jax.ShapeDtypeStruct((N_GY, GROUP, BS), jnp.float32)],
        scratch_shapes=[
            pltpu.SemaphoreType.DMA((N_GY - 1,)),
            pltpu.SemaphoreType.DMA((N_GY - 1,)),
            pltpu.SemaphoreType.DMA((2,)),
            pltpu.SemaphoreType.DMA((2,)),
            pltpu.SemaphoreType.DMA(()),
        ],
        compiler_params=pltpu.CompilerParams(
            collective_id=1, has_side_effects=True, vmem_limit_bytes=16 << 20
        ),
        name="deliver",
    )(low, high, dual)


def total_kernel(
    own, above_in, below_in, got, pot, target, dual_hbm, moments_hbm, new_pot_hbm,
    moments, new_pot, dual_pot, sems,
):
    parts = 4
    size = 4 * SB // parts
    sends = []
    for q in range(parts):

        @pl.loop(0, SB // 16 // parts)
        def _(i):
            at = pl.multiple_of(q * size + i * 64, 64)
            moments[pl.ds(at, 64), :] = (
                own[pl.ds(at, 64), :] + above_in[pl.ds(at, 64), :] + below_in[pl.ds(at, 64), :]
            )
            for j in range(2):
                rows = pl.ds(pl.multiple_of(q * (size // 4) + i * 16, 16) + 8 * j, 8)
                mass = moments[pl.ds(at + 32 * j, 8, stride=4), :]
                new_pot[rows, :] = pot[rows, :] + STEP * (target[rows, :] - mass)

        some = pl.ds(q * size, size)
        sends.append(pltpu.make_async_copy(moments.at[some], moments_hbm.at[some], sems.at[q]))
        sends[-1].start()
    sends.append(pltpu.make_async_copy(new_pot, new_pot_hbm, sems.at[parts]))
    sends[-1].start()
    row = lax.broadcasted_iota(jnp.int32, (ROWS, BS), 0).astype(jnp.float32)
    total = None
    for half in range(2):
        fill = None
        for j in range(4):
            index = got[4 * half + j, PAIR_CAP : PAIR_CAP + 1, :]
            fill = index if fill is None else jnp.maximum(fill, index)
        hot = bf(jnp.where(row == fill, 1.0, 0.0))
        rest = jnp.concatenate([got[4 * half + j, :PAIR_CAP, :] for j in range(4)], axis=0)
        for _ in range(3):
            piece = bf(rest)
            rest = rest - f32(piece)
            term = jnp.dot(hot, piece, preferred_element_type=jnp.float32)
            total = term if total is None else total + term
    dual_pot[...] = total
    sends.append(pltpu.make_async_copy(dual_pot, dual_hbm, sems.at[parts + 1]))
    sends[-1].start()
    for send in sends:
        send.wait()


def total(own, above_in, below_in, got, pot, target):
    shapes = [(ROWS, BS), (4 * SB, BS), (SB, BS)]
    return pl.pallas_call(
        total_kernel,
        in_specs=[VMEM] * 6,
        out_specs=[HBM] * 3,
        out_shape=[jax.ShapeDtypeStruct(shape, jnp.float32) for shape in shapes],
        scratch_shapes=[
            pltpu.VMEM((4 * SB, BS), jnp.float32),
            pltpu.VMEM((SB, BS), jnp.float32),
            pltpu.VMEM((ROWS, BS), jnp.float32),
            pltpu.SemaphoreType.DMA((6,)),
        ],
        compiler_params=pltpu.CompilerParams(vmem_limit_bytes=16 << 20),
        name="total",
    )(own, above_in, below_in, got, pot, target)


BUFFERS = ("split", "xat", "part", "top", "f8")


def work_kernel(
    pidx, listed, vox_hbm, mass_hbm, ypool,
    low_out, own_out, high_out, dual, mom, vox, mass, sems, *scratch,
):
    loads = [
        pltpu.make_async_copy(vox_hbm, vox, sems.at[0]),
        pltpu.make_async_copy(mass_hbm, mass, sems.at[1]),
    ]
    for load in loads:
        load.start()
    first_lane = (lax.axis_index("gy") & 3) * PAIR_CAP
    n = listed[2, 0]

    @pl.loop(0, POOL // 16)
    def _(i):
        for j in range(16):
            mom[i * 16 + j] = jnp.zeros((8, BS), jnp.float32)

    for load in loads:
        load.wait()
    size = len(BUFFERS)
    bufs = [dict(zip(BUFFERS, scratch[i * size : (i + 1) * size])) for i in range(SLOTS * TOGETHER)]
    lane = lax.broadcasted_iota(jnp.int32, (1, BS), 1)
    dual[...] = jnp.full(dual.shape, -1.0, jnp.float32)

    def prepare(t, b):
        s = listed[0, t]
        x = vox[pl.ds(s, 3, stride=VB), :] - 0.5
        xh = f32(bf(x))
        xl = x - xh
        tops = [f32(ypool[pidx[s * KC + k], 0:8, :]) for k in range(KC)]
        while len(tops) > 1:
            tops = [jnp.maximum(a, c) for a, c in zip(tops[::2], tops[1::2])]
        top = jnp.max(tops[0][3:4], axis=1, keepdims=True)
        top = jnp.broadcast_to(top, (1, BS))
        one = jnp.ones((1, BS), jnp.float32)
        xa = jnp.concatenate([xh, one, xh, one, xl, one, xl, -top], axis=0)
        b["xat"][...] = bf(xa.T)
        b["top"][0:1, :] = top

    def score(t, b, c):
        s = listed[0, t]
        y = [ypool[pidx[s * KC + 2 * c + j]] for j in range(2)]
        return jnp.dot(
            b["xat"][...], jnp.concatenate(y, axis=1), preferred_element_type=jnp.float32
        )

    def spread(t, b, c):
        s = listed[0, t]
        e = jnp.concatenate([b["split"][2 * c], b["split"][2 * c + 1]], axis=1)
        m = jnp.dot(b["f8"][...], e, preferred_element_type=jnp.float32)
        for j in range(2):
            mom[pidx[s * KC + 2 * c + j]] += m[:, j * BS : (j + 1) * BS]

    def weigh(sc, b, c, part):
        e = jnp.exp2(sc)
        eh = bf(e)
        el = bf(e - f32(eh))
        for j in range(2):
            b["split"][2 * c + j, 0:BS, :] = eh[:, j * BS : (j + 1) * BS]
            b["split"][2 * c + j, BS:, :] = el[:, j * BS : (j + 1) * BS]
        p = e[:, :BS] + e[:, BS:]
        return p if part is None else part + p

    def weigh_and_spread(new, old):
        parts = [None] * len(new)
        for c in range(KC // 2):
            scores = [score(t, b, c) for t, b in new]
            for t, b in old:
                spread(t, b, c)
            parts = [weigh(sc, b, c, p) for sc, (t, b), p in zip(scores, new, parts)]
        for p, (t, b) in zip(parts, new):
            b["part"][...] = p

    def norm(t, b):
        s = listed[0, t]
        d = jnp.sum(b["part"][...].T, axis=0, keepdims=True)
        xr = vox[pl.ds(s, 3, stride=VB), :]
        x = xr - 0.5
        sq = jnp.sum(x * x, axis=0, keepdims=True)
        where = listed[1, t]
        top_row = (where >> 16) * GROUP
        rank = (where >> 8) & 255
        mark = pl.ds(top_row + PAIR_CAP, 1)
        dual[mark, :] = jnp.where(
            lane == first_lane + rank, (where & 255).astype(jnp.float32), dual[mark, :]
        )
        dual[pl.ds(top_row + rank, 1), :] = (1.0 / EPS) * sq - LN2 * (b["top"][0:1, :] + jnp.log2(d))
        w = mass[pl.ds(s, 1), :] / d
        f = jnp.concatenate([w, xr * w], axis=0)
        fh = f32(bf(f))
        f8 = bf(jnp.concatenate([fh, f - fh], axis=0))
        b["f8"][...] = jnp.concatenate([f8, f8], axis=1)

    def step(g, slot, valid):
        def blocks(lag):
            if not valid(lag):
                return []
            first = ((slot - lag) % SLOTS) * TOGETHER
            return [((g - lag) * TOGETHER + u, bufs[first + u]) for u in range(TOGETHER)]

        for t, b in blocks(0):
            prepare(t, b)
        new, old = blocks(1), blocks(3)
        for u in range(0, TOGETHER, 2):
            weigh_and_spread(new[u : u + 2], old[u : u + 2])
        for t, b in blocks(2):
            norm(t, b)

    groups = n // TOGETHER

    @pl.when(n > 0)
    def _():
        for g in range(SLOTS):
            step(g, g, lambda lag: lag <= g)

        @pl.loop(0, (groups - SLOTS) // SLOTS)
        def _(h):
            for u in range(SLOTS):
                step(SLOTS + SLOTS * h + u, u, lambda lag: True)

        for e in range(3):
            step(groups + e, e, lambda lag: lag > e)

    for q, out in enumerate((low_out, own_out, high_out)):

        @pl.loop(0, SB // 16)
        def _(g):
            for j in range(16):
                m = mom[q * SB + g * 16 + j]
                out[g * 16 + j] = m[0:4] + m[4:8]


def work(pidx, listed, vox, mass, ypool):
    moments = jax.ShapeDtypeStruct((SB, 4, BS), jnp.float32)
    scratch = [
        pltpu.VMEM((POOL, 8, BS), jnp.float32),
        pltpu.VMEM((3 * VB, BS), jnp.float32),
        pltpu.VMEM((VB, BS), jnp.float32),
        pltpu.SemaphoreType.DMA((2,)),
    ]
    scratch += [
        pltpu.VMEM((KC, 2 * BS, BS), jnp.bfloat16),
        pltpu.VMEM((BS, 16), jnp.bfloat16),
        pltpu.VMEM((BS, BS), jnp.float32),
        pltpu.VMEM((8, BS), jnp.float32),
        pltpu.VMEM((8, 2 * BS), jnp.bfloat16),
    ] * (SLOTS * TOGETHER)
    return pl.pallas_call(
        work_kernel,
        in_specs=[SMEM] * 2 + [HBM] * 2 + [VMEM],
        out_specs=[VMEM] * 4,
        out_shape=[moments] * 3 + [jax.ShapeDtypeStruct((N_GY * GROUP, BS), jnp.float32)],
        scratch_shapes=scratch,
        compiler_params=pltpu.CompilerParams(vmem_limit_bytes=32 << 20),
        name="work",
    )(
        pidx,
        listed,
        pltpu.with_memory_space_constraint(vox, pltpu.HBM),
        pltpu.with_memory_space_constraint(mass, pltpu.HBM),
        ypool,
    )


def on_device(
    voxel_xyz, voxel_mass, candidates, offload_plan, seed_xyz, seed_pot, seed_target, seed_home
):
    ypool, pidx, listed = exchange(
        jnp.transpose(seed_xyz, (1, 0, 2)),
        seed_pot,
        candidates.T,
        seed_home,
        offload_plan.reshape(VB // BS, BS),
    )
    vox = jnp.transpose(voxel_xyz, (1, 0, 2)).reshape(3 * VB, BS)
    low, own, high, dual = work(pidx, listed, vox, voxel_mass, ypool)
    flat = lambda m: m.reshape(4 * SB, BS)
    above_in, below_in, got = deliver(flat(low), flat(high), dual.reshape(N_GY, GROUP, BS))
    dual_pot, moments, new_pot = total(
        flat(own), above_in, below_in, got, seed_pot, seed_target
    )
    return (dual_pot, moments.reshape(SB, 4, BS), new_pot)


def solution(mesh):
    return jax.shard_map(
        on_device,
        mesh=mesh,
        in_specs=(
            P(("gx", "gy"), None, None),
            P(("gx", "gy"), None),
            P(("gx", "gy"), None),
            P(("gx", "gy")),
            P(("gx", "gy"), None, None),
            P(("gx", "gy"), None),
            P(("gx", "gy"), None),
            P(),
        ),
        out_specs=(P(("gx", "gy"), None), P(("gx", "gy"), None, None), P(("gx", "gy"), None)),
        check_vma=False,
    )
```

```python
import math

import jax
import jax.numpy as jnp
from jax import lax
from jax.experimental import pallas as pl
from jax.experimental.pallas import tpu as pltpu
from jax.sharding import PartitionSpec as P

BS = 128
KC = 8
PAIR_CAP = 32
VB = 256
SB = 512
POOL = 3 * SB
N_GX = 16
N_GY = 8
ROWS = 128
GROUP = 40
SLOTS = 4
TOGETHER = 4
CHUNKS = 4

EPS = 0.05
STEP = 0.5
LOG2E = math.log2(math.e)
LN2 = math.log(2.0)

VMEM = pl.BlockSpec(memory_space=pltpu.VMEM)
SMEM = pl.BlockSpec(memory_space=pltpu.SMEM)
HBM = pl.BlockSpec(memory_space=pltpu.HBM)
MESH = pl.DeviceIdType.MESH


def bf(x):
    return x.astype(jnp.bfloat16)


def f32(x):
    return x.astype(jnp.float32)


def meet(peers):
    barrier = pltpu.get_barrier_semaphore()
    for peer in peers:
        pl.semaphore_signal(barrier, inc=1, device_id=peer, device_id_type=MESH)
    pl.semaphore_wait(barrier, len(peers))


def exchange_kernel(
    xyz_hbm, pot_hbm, cand_hbm, home_hbm, plan_hbm, vox_hbm, ypool, tops, xats, pidx, listed,
    xyz, pot, plane, cand, home, plan, vox, load_sem, send_sem, recv_sem,
):
    x, g = lax.axis_index("gx"), lax.axis_index("gy")
    below, above = (x + N_GX - 1) % N_GX, (x + 1) % N_GX
    pairs = (
        (xyz_hbm, xyz.at[1]), (pot_hbm, pot.at[1]), (cand_hbm, cand), (home_hbm, home),
        (plan_hbm, plan), (vox_hbm, vox),
    )
    loads = [pltpu.make_async_copy(a, b, load_sem.at[i]) for i, (a, b) in enumerate(pairs)]
    for load in loads:
        load.start()
    meet([(below, g), (above, g)])
    copies = []
    for q in range(CHUNKS):
        some = pl.ds(q * (SB // CHUNKS), SB // CHUNKS)
        for way, (slot, peer) in enumerate(((0, above), (2, below))):
            for kind, (source, dest) in enumerate(
                (
                    (xyz_hbm.at[:, some, :], xyz.at[slot, :, some, :]),
                    (pot_hbm.at[some, :], pot.at[slot, some, :]),
                )
            ):
                i = (q * 2 + way) * 2 + kind
                copy = pltpu.make_async_remote_copy(
                    source, dest, send_sem.at[i], recv_sem.at[i],
                    device_id=(peer, g), device_id_type=MESH,
                )
                copy.start()
                copies.append(copy)

    sub = lax.broadcasted_iota(jnp.int32, (8, BS), 0)
    low = sub < 4

    def build(slot, start, count):
        @pl.loop(0, count // 16)
        def _(i):
            at = pl.multiple_of(start + i * 16, 16)
            square = None
            for c in range(3):
                y = xyz[slot, c, pl.ds(at, 16), :] - 0.5
                plane[c * 16 : (c + 1) * 16, :] = (2.0 * LOG2E / EPS) * y
                square = y * y if square is None else square + y * y
            offset = LOG2E * (pot[slot, pl.ds(at, 16), :] - (1.0 / EPS) * square)
            plane[48:64, :] = offset
            top = f32(bf(jnp.max(offset, axis=1, keepdims=True)))
            tops[pl.ds(slot * SB + at, 16), :] = jnp.broadcast_to(top, (16, BS))
            for j in range(16):
                t = plane[pl.ds(j, 4, stride=16), :]
                a = jnp.concatenate([t, t], axis=0)
                hi = f32(bf(a))
                mid = f32(bf(a - hi))
                first = jnp.where(low, hi, mid)
                second = jnp.where(sub == 3, a - hi - mid, jnp.where(sub == 7, 0.0, first))
                ypool[slot * SB + at + j] = bf(jnp.concatenate([first, second], axis=0))

    loads[0].wait()
    loads[1].wait()
    build(1, 0, SB)
    loads[4].wait()
    loads[5].wait()

    @pl.loop(0, VB // 4)
    def _(h):
        for u in range(4):
            v = h * 4 + u
            x = vox[pl.ds(v, 3, stride=VB), :] - 0.5
            xh = f32(bf(x))
            xl = x - xh
            one = jnp.ones((1, BS), jnp.float32)
            xa = jnp.concatenate([xh, one, xh, one, xl, one, xl, one], axis=0)
            xats[v] = bf(xa.T)

    p = jnp.concatenate([plan[0:1, :], plan[1:2, :]], axis=1)
    wide = lambda axis, rows: lax.broadcasted_iota(jnp.int32, (rows, VB), axis)
    taken = jnp.broadcast_to(p >= 0, (8, VB))
    dest = jnp.broadcast_to((p >> 7) & 7, (8, VB))
    one_hot = jnp.where(taken, jnp.where(dest == wide(0, 8), 1.0, 0.0), 0.0)
    before = jnp.where(wide(0, VB) < wide(1, VB), 1.0, 0.0)
    earlier = jnp.dot(bf(one_hot), bf(before), preferred_element_type=jnp.float32)
    rank = jnp.sum(earlier * one_hot, axis=0, keepdims=True)
    place = jnp.sum(earlier, axis=0, keepdims=True)
    place = jnp.where(p >= 0, place, -1.0)
    chosen = jnp.where(place == wide(0, VB).astype(jnp.float32), 1.0, 0.0)
    facts = [
        wide(1, 1).astype(jnp.float32),
        ((p >> 7) & 7).astype(jnp.float32),
        rank,
        (p & 127).astype(jnp.float32),
        jnp.zeros((4, VB), jnp.float32),
    ]
    facts = lax.dot_general(
        bf(jnp.concatenate(facts, axis=0)),
        bf(chosen),
        (((1,), (1,)), ((), ())),
        preferred_element_type=jnp.float32,
    ).astype(jnp.int32)
    count = jnp.sum(one_hot, axis=(0, 1), keepdims=True).astype(jnp.int32)
    listed[0:1, :] = facts[0:1]
    listed[1:2, :] = (facts[1:2] << 16) | (facts[2:3] << 8) | facts[3:4]
    listed[2:8, :] = jnp.broadcast_to(count, (6, VB))
    loads[2].wait()
    loads[3].wait()

    @pl.loop(0, VB // 2)
    def _(h):
        for u in range(2):
            v = 2 * h + u
            for k in range(KC):
                s = home[cand[k, v]]
                pidx[v * KC + k] = ((((s >> 12) - x + 1) & 15) << 9) | (s & 511)

    for q in range(CHUNKS):
        for copy in copies[4 * q : 4 * q + 4]:
            copy.wait_recv()
        for slot in (0, 2):
            build(slot, q * (SB // CHUNKS), SB // CHUNKS)
    for copy in copies:
        copy.wait_send()


def exchange(xyz, pot, cand, home, plan, vox):
    return pl.pallas_call(
        exchange_kernel,
        in_specs=[HBM] * 6,
        out_specs=[VMEM, VMEM, VMEM, SMEM, VMEM],
        out_shape=[
            jax.ShapeDtypeStruct((POOL, 16, BS), jnp.bfloat16),
            jax.ShapeDtypeStruct((POOL, BS), jnp.float32),
            jax.ShapeDtypeStruct((VB, BS, 16), jnp.bfloat16),
            jax.ShapeDtypeStruct((VB * KC,), jnp.int32),
            jax.ShapeDtypeStruct((8, VB), jnp.int32),
        ],
        scratch_shapes=[
            pltpu.VMEM((3, 3, SB, BS), jnp.float32),
            pltpu.VMEM((3, SB, BS), jnp.float32),
            pltpu.VMEM((64, BS), jnp.float32),
            pltpu.SMEM((KC, VB), jnp.int32),
            pltpu.SMEM((N_GX * N_GY * SB,), jnp.int32),
            pltpu.VMEM((VB // BS, BS), jnp.int32),
            pltpu.VMEM((3 * VB, BS), jnp.float32),
            pltpu.SemaphoreType.DMA((6,)),
            pltpu.SemaphoreType.DMA((4 * CHUNKS,)),
            pltpu.SemaphoreType.DMA((4 * CHUNKS,)),
        ],
        compiler_params=pltpu.CompilerParams(
            collective_id=0, has_side_effects=True, vmem_limit_bytes=24 << 20
        ),
        name="exchange",
    )(*(pltpu.with_memory_space_constraint(a, pltpu.HBM) for a in (xyz, pot, cand, home, plan, vox)))


def deliver_kernel(
    low, high, dual, above_in, below_in, got, dual_send, dual_recv, send_sem, recv_sem, own_sem
):
    x, g = lax.axis_index("gx"), lax.axis_index("gy")
    below, above = (x + N_GX - 1) % N_GX, (x + 1) % N_GX
    others = [(g + d) % N_GY for d in range(1, N_GY)]
    meet([(below, g), (above, g)] + [(x, peer) for peer in others])
    copies = [
        pltpu.make_async_remote_copy(
            low, above_in, send_sem.at[0], recv_sem.at[0],
            device_id=(below, g), device_id_type=MESH,
        ),
        pltpu.make_async_remote_copy(
            high, below_in, send_sem.at[1], recv_sem.at[1],
            device_id=(above, g), device_id_type=MESH,
        ),
    ]
    for d, peer in enumerate(others):
        copies.append(
            pltpu.make_async_remote_copy(
                dual.at[peer], got.at[g], dual_send.at[d], dual_recv.at[d],
                device_id=(x, peer), device_id_type=MESH,
            )
        )
    keep = pltpu.make_async_copy(dual.at[g], got.at[g], own_sem)
    for copy in copies:
        copy.start()
    keep.start()
    keep.wait()
    for copy in copies:
        copy.wait()


def deliver(low, high, dual):
    moments = jax.ShapeDtypeStruct((4 * SB, BS), jnp.float32)
    return pl.pallas_call(
        deliver_kernel,
        in_specs=[VMEM] * 3,
        out_specs=[VMEM] * 3,
        out_shape=[moments] * 2 + [jax.ShapeDtypeStruct((N_GY, GROUP, BS), jnp.float32)],
        scratch_shapes=[
            pltpu.SemaphoreType.DMA((N_GY - 1,)),
            pltpu.SemaphoreType.DMA((N_GY - 1,)),
            pltpu.SemaphoreType.DMA((2,)),
            pltpu.SemaphoreType.DMA((2,)),
            pltpu.SemaphoreType.DMA(()),
        ],
        compiler_params=pltpu.CompilerParams(
            collective_id=1, has_side_effects=True, vmem_limit_bytes=16 << 20
        ),
        name="deliver",
    )(low, high, dual)


def total_kernel(
    own, above_in, below_in, got, pot, target, dual_hbm, moments_hbm, new_pot_hbm,
    moments, new_pot, dual_pot, sems,
):
    parts = 4
    size = 4 * SB // parts
    sends = []
    for q in range(parts):

        @pl.loop(0, SB // 16 // parts)
        def _(i):
            at = pl.multiple_of(q * size + i * 64, 64)
            moments[pl.ds(at, 64), :] = (
                own[pl.ds(at, 64), :] + above_in[pl.ds(at, 64), :] + below_in[pl.ds(at, 64), :]
            )
            for j in range(2):
                rows = pl.ds(pl.multiple_of(q * (size // 4) + i * 16, 16) + 8 * j, 8)
                mass = moments[pl.ds(at + 32 * j, 8, stride=4), :]
                new_pot[rows, :] = pot[rows, :] + STEP * (target[rows, :] - mass)

        some = pl.ds(q * size, size)
        sends.append(pltpu.make_async_copy(moments.at[some], moments_hbm.at[some], sems.at[q]))
        sends[-1].start()
    sends.append(pltpu.make_async_copy(new_pot, new_pot_hbm, sems.at[parts]))
    sends[-1].start()
    row = lax.broadcasted_iota(jnp.int32, (ROWS, BS), 0).astype(jnp.float32)
    total = None
    for half in range(2):
        fill = None
        for j in range(4):
            index = got[4 * half + j, PAIR_CAP : PAIR_CAP + 1, :]
            fill = index if fill is None else jnp.maximum(fill, index)
        hot = bf(jnp.where(row == fill, 1.0, 0.0))
        rest = jnp.concatenate([got[4 * half + j, :PAIR_CAP, :] for j in range(4)], axis=0)
        for _ in range(3):
            piece = bf(rest)
            rest = rest - f32(piece)
            term = jnp.dot(hot, piece, preferred_element_type=jnp.float32)
            total = term if total is None else total + term
    dual_pot[...] = total
    sends.append(pltpu.make_async_copy(dual_pot, dual_hbm, sems.at[parts + 1]))
    sends[-1].start()
    for send in sends:
        send.wait()


def total(own, above_in, below_in, got, pot, target):
    shapes = [(ROWS, BS), (4 * SB, BS), (SB, BS)]
    return pl.pallas_call(
        total_kernel,
        in_specs=[VMEM] * 6,
        out_specs=[HBM] * 3,
        out_shape=[jax.ShapeDtypeStruct(shape, jnp.float32) for shape in shapes],
        scratch_shapes=[
            pltpu.VMEM((4 * SB, BS), jnp.float32),
            pltpu.VMEM((SB, BS), jnp.float32),
            pltpu.VMEM((ROWS, BS), jnp.float32),
            pltpu.SemaphoreType.DMA((6,)),
        ],
        compiler_params=pltpu.CompilerParams(vmem_limit_bytes=16 << 20),
        name="total",
    )(own, above_in, below_in, got, pot, target)


BUFFERS = ("split", "shift", "part", "top", "f8")


def work_kernel(
    pidx, listed, vox_hbm, mass_hbm, ypool, tops, xats,
    low_out, own_out, high_out, dual, mom, vox, mass, sems, *scratch,
):
    loads = [
        pltpu.make_async_copy(vox_hbm, vox, sems.at[0]),
        pltpu.make_async_copy(mass_hbm, mass, sems.at[1]),
    ]
    for load in loads:
        load.start()
    first_lane = (lax.axis_index("gy") & 3) * PAIR_CAP
    n = listed[2, 0]

    @pl.loop(0, POOL // 16)
    def _(i):
        for j in range(16):
            mom[i * 16 + j] = jnp.zeros((8, BS), jnp.float32)

    for load in loads:
        load.wait()
    size = len(BUFFERS)
    bufs = [dict(zip(BUFFERS, scratch[i * size : (i + 1) * size])) for i in range(SLOTS * TOGETHER)]
    lane = lax.broadcasted_iota(jnp.int32, (1, BS), 1)
    dual[...] = jnp.full(dual.shape, -1.0, jnp.float32)

    last = lax.broadcasted_iota(jnp.int32, (16, BS), 0) == 15

    def prepare(t, b):
        s = listed[0, t]
        high = [tops[pl.ds(pidx[s * KC + k], 1), :] for k in range(KC)]
        while len(high) > 1:
            high = [jnp.maximum(a, c) for a, c in zip(high[::2], high[1::2])]
        b["top"][0:1, :] = high[0]
        b["shift"][...] = bf(jnp.where(last, -high[0], 0.0))

    def score(t, b, c):
        s = listed[0, t]
        y = [ypool[pidx[s * KC + 2 * c + j]] + b["shift"][...] for j in range(2)]
        return jnp.dot(
            xats[s], jnp.concatenate(y, axis=1), preferred_element_type=jnp.float32
        )

    def spread(t, b, c):
        s = listed[0, t]
        e = jnp.concatenate([b["split"][2 * c], b["split"][2 * c + 1]], axis=1)
        m = jnp.dot(b["f8"][...], e, preferred_element_type=jnp.float32)
        for j in range(2):
            mom[pidx[s * KC + 2 * c + j]] += m[:, j * BS : (j + 1) * BS]

    def weigh(sc, b, c, part):
        e = jnp.exp2(sc)
        eh = bf(e)
        el = bf(e - f32(eh))
        for j in range(2):
            b["split"][2 * c + j, 0:BS, :] = eh[:, j * BS : (j + 1) * BS]
            b["split"][2 * c + j, BS:, :] = el[:, j * BS : (j + 1) * BS]
        p = e[:, :BS] + e[:, BS:]
        return p if part is None else part + p

    def weigh_and_spread(new, old):
        parts = [None] * len(new)
        for c in range(KC // 2):
            scores = [score(t, b, c) for t, b in new]
            for t, b in old:
                spread(t, b, c)
            parts = [weigh(sc, b, c, p) for sc, (t, b), p in zip(scores, new, parts)]
        for p, (t, b) in zip(parts, new):
            b["part"][...] = p

    def norm(t, b):
        s = listed[0, t]
        d = jnp.sum(b["part"][...].T, axis=0, keepdims=True)
        xr = vox[pl.ds(s, 3, stride=VB), :]
        x = xr - 0.5
        sq = jnp.sum(x * x, axis=0, keepdims=True)
        where = listed[1, t]
        top_row = (where >> 16) * GROUP
        rank = (where >> 8) & 255
        mark = pl.ds(top_row + PAIR_CAP, 1)
        dual[mark, :] = jnp.where(
            lane == first_lane + rank, (where & 255).astype(jnp.float32), dual[mark, :]
        )
        dual[pl.ds(top_row + rank, 1), :] = (1.0 / EPS) * sq - LN2 * (b["top"][0:1, :] + jnp.log2(d))
        w = mass[pl.ds(s, 1), :] / d
        f = jnp.concatenate([w, xr * w], axis=0)
        fh = f32(bf(f))
        f8 = bf(jnp.concatenate([fh, f - fh], axis=0))
        b["f8"][...] = jnp.concatenate([f8, f8], axis=1)

    def step(g, slot, valid):
        def blocks(lag):
            if not valid(lag):
                return []
            first = ((slot - lag) % SLOTS) * TOGETHER
            return [((g - lag) * TOGETHER + u, bufs[first + u]) for u in range(TOGETHER)]

        for t, b in blocks(0):
            prepare(t, b)
        new, old = blocks(1), blocks(3)
        for u in range(0, TOGETHER, 2):
            weigh_and_spread(new[u : u + 2], old[u : u + 2])
        for t, b in blocks(2):
            norm(t, b)

    groups = n // TOGETHER

    @pl.when(n > 0)
    def _():
        for g in range(SLOTS):
            step(g, g, lambda lag: lag <= g)

        @pl.loop(0, (groups - SLOTS) // SLOTS)
        def _(h):
            for u in range(SLOTS):
                step(SLOTS + SLOTS * h + u, u, lambda lag: True)

        for e in range(3):
            step(groups + e, e, lambda lag: lag > e)

    for q, out in enumerate((low_out, own_out, high_out)):

        @pl.loop(0, SB // 16)
        def _(g):
            for j in range(16):
                m = mom[q * SB + g * 16 + j]
                out[g * 16 + j] = m[0:4] + m[4:8]


def work(pidx, listed, vox, mass, ypool, tops, xats):
    moments = jax.ShapeDtypeStruct((SB, 4, BS), jnp.float32)
    scratch = [
        pltpu.VMEM((POOL, 8, BS), jnp.float32),
        pltpu.VMEM((3 * VB, BS), jnp.float32),
        pltpu.VMEM((VB, BS), jnp.float32),
        pltpu.SemaphoreType.DMA((2,)),
    ]
    scratch += [
        pltpu.VMEM((KC, 2 * BS, BS), jnp.bfloat16),
        pltpu.VMEM((16, BS), jnp.bfloat16),
        pltpu.VMEM((BS, BS), jnp.float32),
        pltpu.VMEM((8, BS), jnp.float32),
        pltpu.VMEM((8, 2 * BS), jnp.bfloat16),
    ] * (SLOTS * TOGETHER)
    return pl.pallas_call(
        work_kernel,
        in_specs=[SMEM] * 2 + [HBM] * 2 + [VMEM] * 3,
        out_specs=[VMEM] * 4,
        out_shape=[moments] * 3 + [jax.ShapeDtypeStruct((N_GY * GROUP, BS), jnp.float32)],
        scratch_shapes=scratch,
        compiler_params=pltpu.CompilerParams(vmem_limit_bytes=32 << 20),
        name="work",
    )(
        pidx,
        listed,
        pltpu.with_memory_space_constraint(vox, pltpu.HBM),
        pltpu.with_memory_space_constraint(mass, pltpu.HBM),
        ypool,
        tops,
        xats,
    )


def on_device(
    voxel_xyz, voxel_mass, candidates, offload_plan, seed_xyz, seed_pot, seed_target, seed_home
):
    vox = jnp.transpose(voxel_xyz, (1, 0, 2)).reshape(3 * VB, BS)
    ypool, tops, xats, pidx, listed = exchange(
        jnp.transpose(seed_xyz, (1, 0, 2)),
        seed_pot,
        candidates.T,
        seed_home,
        offload_plan.reshape(VB // BS, BS),
        vox,
    )
    low, own, high, dual = work(pidx, listed, vox, voxel_mass, ypool, tops, xats)
    flat = lambda m: m.reshape(4 * SB, BS)
    above_in, below_in, got = deliver(flat(low), flat(high), dual.reshape(N_GY, GROUP, BS))
    dual_pot, moments, new_pot = total(
        flat(own), above_in, below_in, got, seed_pot, seed_target
    )
    return (dual_pot, moments.reshape(SB, 4, BS), new_pot)


def solution(mesh):
    return jax.shard_map(
        on_device,
        mesh=mesh,
        in_specs=(
            P(("gx", "gy"), None, None),
            P(("gx", "gy"), None),
            P(("gx", "gy"), None),
            P(("gx", "gy")),
            P(("gx", "gy"), None, None),
            P(("gx", "gy"), None),
            P(("gx", "gy"), None),
            P(),
        ),
        out_specs=(P(("gx", "gy"), None), P(("gx", "gy"), None, None), P(("gx", "gy"), None)),
        check_vma=False,
    )
```

```python
import math

import jax
import jax.numpy as jnp
from jax import lax
from jax.experimental import pallas as pl
from jax.experimental.pallas import tpu as pltpu
from jax.sharding import PartitionSpec as P

BS = 128
KC = 8
PAIR_CAP = 32
VB = 256
SB = 512
POOL = 3 * SB
N_GX = 16
N_GY = 8
ROWS = 128
GROUP = 40
SLOTS = 4
TOGETHER = 4
CHUNKS = 8

EPS = 0.05
STEP = 0.5
LOG2E = math.log2(math.e)
LN2 = math.log(2.0)

VMEM = pl.BlockSpec(memory_space=pltpu.VMEM)
SMEM = pl.BlockSpec(memory_space=pltpu.SMEM)
HBM = pl.BlockSpec(memory_space=pltpu.HBM)
MESH = pl.DeviceIdType.MESH


def bf(x):
    return x.astype(jnp.bfloat16)


def f32(x):
    return x.astype(jnp.float32)


def meet(peers):
    barrier = pltpu.get_barrier_semaphore()
    for peer in peers:
        pl.semaphore_signal(barrier, inc=1, device_id=peer, device_id_type=MESH)
    pl.semaphore_wait(barrier, len(peers))


def exchange_kernel(
    xyz_hbm, pot_hbm, cand_hbm, home_hbm, plan_hbm, ypool, pidx, listed,
    xyz, pot, plane, cand, home, plan, load_sem, send_sem, recv_sem,
):
    x, g = lax.axis_index("gx"), lax.axis_index("gy")
    below, above = (x + N_GX - 1) % N_GX, (x + 1) % N_GX
    pairs = (
        (xyz_hbm, xyz.at[1]), (pot_hbm, pot.at[1]), (cand_hbm, cand), (home_hbm, home),
        (plan_hbm, plan),
    )
    loads = [pltpu.make_async_copy(a, b, load_sem.at[i]) for i, (a, b) in enumerate(pairs)]
    for load in loads:
        load.start()
    meet([(below, g), (above, g)])
    copies = []
    for q in range(CHUNKS):
        some = pl.ds(q * (SB // CHUNKS), SB // CHUNKS)
        for way, (slot, peer) in enumerate(((0, above), (2, below))):
            for kind, (source, dest) in enumerate(
                (
                    (xyz_hbm.at[:, some, :], xyz.at[slot, :, some, :]),
                    (pot_hbm.at[some, :], pot.at[slot, some, :]),
                )
            ):
                i = (q * 2 + way) * 2 + kind
                copy = pltpu.make_async_remote_copy(
                    source, dest, send_sem.at[i], recv_sem.at[i],
                    device_id=(peer, g), device_id_type=MESH,
                )
                copy.start()
                copies.append(copy)

    sub = lax.broadcasted_iota(jnp.int32, (8, BS), 0)
    low = sub < 4

    def build(slot, start, count):
        @pl.loop(0, count // 16)
        def _(i):
            at = pl.multiple_of(start + i * 16, 16)
            square = None
            for c in range(3):
                y = xyz[slot, c, pl.ds(at, 16), :] - 0.5
                plane[c * 16 : (c + 1) * 16, :] = (2.0 * LOG2E / EPS) * y
                square = y * y if square is None else square + y * y
            plane[48:64, :] = LOG2E * (pot[slot, pl.ds(at, 16), :] - (1.0 / EPS) * square)
            for j in range(16):
                t = plane[pl.ds(j, 4, stride=16), :]
                a = jnp.concatenate([t, t], axis=0)
                hi = f32(bf(a))
                mid = f32(bf(a - hi))
                first = jnp.where(low, hi, mid)
                second = jnp.where(sub == 3, a - hi - mid, jnp.where(sub == 7, 1.0, first))
                ypool[slot * SB + at + j] = bf(jnp.concatenate([first, second], axis=0))

    loads[0].wait()
    loads[1].wait()
    build(1, 0, SB)
    loads[4].wait()
    p = jnp.concatenate([plan[0:1, :], plan[1:2, :]], axis=1)
    wide = lambda axis, rows: lax.broadcasted_iota(jnp.int32, (rows, VB), axis)
    taken = jnp.broadcast_to(p >= 0, (8, VB))
    dest = jnp.broadcast_to((p >> 7) & 7, (8, VB))
    one_hot = jnp.where(taken, jnp.where(dest == wide(0, 8), 1.0, 0.0), 0.0)
    before = jnp.where(wide(0, VB) < wide(1, VB), 1.0, 0.0)
    earlier = jnp.dot(bf(one_hot), bf(before), preferred_element_type=jnp.float32)
    rank = jnp.sum(earlier * one_hot, axis=0, keepdims=True)
    place = jnp.sum(earlier, axis=0, keepdims=True)
    place = jnp.where(p >= 0, place, -1.0)
    chosen = jnp.where(place == wide(0, VB).astype(jnp.float32), 1.0, 0.0)
    facts = [
        wide(1, 1).astype(jnp.float32),
        ((p >> 7) & 7).astype(jnp.float32),
        rank,
        (p & 127).astype(jnp.float32),
        jnp.zeros((4, VB), jnp.float32),
    ]
    facts = lax.dot_general(
        bf(jnp.concatenate(facts, axis=0)),
        bf(chosen),
        (((1,), (1,)), ((), ())),
        preferred_element_type=jnp.float32,
    ).astype(jnp.int32)
    count = jnp.sum(one_hot, axis=(0, 1), keepdims=True).astype(jnp.int32)
    listed[0:1, :] = facts[0:1]
    listed[1:2, :] = (facts[1:2] << 16) | (facts[2:3] << 8) | facts[3:4]
    listed[2:8, :] = jnp.broadcast_to(count, (6, VB))
    loads[2].wait()
    loads[3].wait()

    @pl.loop(0, VB // 2)
    def _(h):
        for u in range(2):
            v = 2 * h + u
            for k in range(KC):
                s = home[cand[k, v]]
                pidx[v * KC + k] = ((((s >> 12) - x + 1) & 15) << 9) | (s & 511)

    for q in range(CHUNKS):
        for copy in copies[4 * q : 4 * q + 4]:
            copy.wait_recv()
        for slot in (0, 2):
            build(slot, q * (SB // CHUNKS), SB // CHUNKS)
    for copy in copies:
        copy.wait_send()


def exchange(xyz, pot, cand, home, plan):
    return pl.pallas_call(
        exchange_kernel,
        in_specs=[HBM] * 5,
        out_specs=[VMEM, SMEM, VMEM],
        out_shape=[
            jax.ShapeDtypeStruct((POOL, 16, BS), jnp.bfloat16),
            jax.ShapeDtypeStruct((VB * KC,), jnp.int32),
            jax.ShapeDtypeStruct((8, VB), jnp.int32),
        ],
        scratch_shapes=[
            pltpu.VMEM((3, 3, SB, BS), jnp.float32),
            pltpu.VMEM((3, SB, BS), jnp.float32),
            pltpu.VMEM((64, BS), jnp.float32),
            pltpu.SMEM((KC, VB), jnp.int32),
            pltpu.SMEM((N_GX * N_GY * SB,), jnp.int32),
            pltpu.VMEM((VB // BS, BS), jnp.int32),
            pltpu.SemaphoreType.DMA((5,)),
            pltpu.SemaphoreType.DMA((4 * CHUNKS,)),
            pltpu.SemaphoreType.DMA((4 * CHUNKS,)),
        ],
        compiler_params=pltpu.CompilerParams(
            collective_id=0, has_side_effects=True, vmem_limit_bytes=16 << 20
        ),
        name="exchange",
    )(*(pltpu.with_memory_space_constraint(a, pltpu.HBM) for a in (xyz, pot, cand, home, plan)))


def deliver_kernel(
    low, high, dual, above_in, below_in, dual_pot,
    got, dual_send, dual_recv, send_sem, recv_sem, own_sem,
):
    x, g = lax.axis_index("gx"), lax.axis_index("gy")
    below, above = (x + N_GX - 1) % N_GX, (x + 1) % N_GX
    others = [(g + d) % N_GY for d in range(1, N_GY)]
    meet([(below, g), (above, g)] + [(x, peer) for peer in others])
    copies = [
        pltpu.make_async_remote_copy(
            low, above_in, send_sem.at[0], recv_sem.at[0],
            device_id=(below, g), device_id_type=MESH,
        ),
        pltpu.make_async_remote_copy(
            high, below_in, send_sem.at[1], recv_sem.at[1],
            device_id=(above, g), device_id_type=MESH,
        ),
    ]
    for d, peer in enumerate(others):
        copies.append(
            pltpu.make_async_remote_copy(
                dual.at[peer], got.at[g], dual_send.at[d], dual_recv.at[d],
                device_id=(x, peer), device_id_type=MESH,
            )
        )
    keep = pltpu.make_async_copy(dual.at[g], got.at[g], own_sem)
    for copy in copies:
        copy.start()
    keep.start()
    keep.wait()
    for copy in copies[2:]:
        copy.wait()
    row = lax.broadcasted_iota(jnp.int32, (ROWS, BS), 0).astype(jnp.float32)
    total = None
    for half in range(2):
        fill = None
        for j in range(4):
            index = got[4 * half + j, PAIR_CAP : PAIR_CAP + 1, :]
            fill = index if fill is None else jnp.maximum(fill, index)
        hot = bf(jnp.where(row == fill, 1.0, 0.0))
        rest = jnp.concatenate([got[4 * half + j, :PAIR_CAP, :] for j in range(4)], axis=0)
        for _ in range(3):
            piece = bf(rest)
            rest = rest - f32(piece)
            term = jnp.dot(hot, piece, preferred_element_type=jnp.float32)
            total = term if total is None else total + term
    dual_pot[...] = total
    for copy in copies[:2]:
        copy.wait()


def deliver(low, high, dual):
    moments = jax.ShapeDtypeStruct((4 * SB, BS), jnp.float32)
    return pl.pallas_call(
        deliver_kernel,
        in_specs=[VMEM] * 3,
        out_specs=[VMEM] * 3,
        out_shape=[moments] * 2 + [jax.ShapeDtypeStruct((ROWS, BS), jnp.float32)],
        scratch_shapes=[
            pltpu.VMEM((N_GY, GROUP, BS), jnp.float32),
            pltpu.SemaphoreType.DMA((N_GY - 1,)),
            pltpu.SemaphoreType.DMA((N_GY - 1,)),
            pltpu.SemaphoreType.DMA((2,)),
            pltpu.SemaphoreType.DMA((2,)),
            pltpu.SemaphoreType.DMA(()),
        ],
        compiler_params=pltpu.CompilerParams(
            collective_id=1, has_side_effects=True, vmem_limit_bytes=16 << 20
        ),
        name="deliver",
    )(low, high, dual)


def total_kernel(
    own, above_in, below_in, dual_pot, pot, target, dual_hbm, moments_hbm, new_pot_hbm,
    moments, new_pot, sems,
):
    parts = 4
    size = 4 * SB // parts
    sends = [pltpu.make_async_copy(dual_pot, dual_hbm, sems.at[parts + 1])]
    sends[0].start()
    for q in range(parts):

        @pl.loop(0, SB // 16 // parts)
        def _(i):
            at = pl.multiple_of(q * size + i * 64, 64)
            moments[pl.ds(at, 64), :] = (
                own[pl.ds(at, 64), :] + above_in[pl.ds(at, 64), :] + below_in[pl.ds(at, 64), :]
            )
            for j in range(2):
                rows = pl.ds(pl.multiple_of(q * (size // 4) + i * 16, 16) + 8 * j, 8)
                mass = moments[pl.ds(at + 32 * j, 8, stride=4), :]
                new_pot[rows, :] = pot[rows, :] + STEP * (target[rows, :] - mass)

        some = pl.ds(q * size, size)
        sends.append(pltpu.make_async_copy(moments.at[some], moments_hbm.at[some], sems.at[q]))
        sends[-1].start()
    sends.append(pltpu.make_async_copy(new_pot, new_pot_hbm, sems.at[parts]))
    sends[-1].start()
    for send in sends:
        send.wait()


def total(own, above_in, below_in, dual_pot, pot, target):
    shapes = [(ROWS, BS), (4 * SB, BS), (SB, BS)]
    return pl.pallas_call(
        total_kernel,
        in_specs=[VMEM] * 6,
        out_specs=[HBM] * 3,
        out_shape=[jax.ShapeDtypeStruct(shape, jnp.float32) for shape in shapes],
        scratch_shapes=[
            pltpu.VMEM((4 * SB, BS), jnp.float32),
            pltpu.VMEM((SB, BS), jnp.float32),
            pltpu.SemaphoreType.DMA((6,)),
        ],
        compiler_params=pltpu.CompilerParams(vmem_limit_bytes=16 << 20),
        name="total",
    )(own, above_in, below_in, dual_pot, pot, target)


BUFFERS = ("split", "xat", "part", "top", "f8")


def work_kernel(
    pidx, listed, vox_hbm, mass_hbm, ypool,
    low_out, own_out, high_out, dual, mom, vox, mass, sems, *scratch,
):
    loads = [
        pltpu.make_async_copy(vox_hbm, vox, sems.at[0]),
        pltpu.make_async_copy(mass_hbm, mass, sems.at[1]),
    ]
    for load in loads:
        load.start()
    first_lane = (lax.axis_index("gy") & 3) * PAIR_CAP
    n = listed[2, 0]

    @pl.loop(0, POOL // 16)
    def _(i):
        for j in range(16):
            mom[i * 16 + j] = jnp.zeros((8, BS), jnp.float32)

    for load in loads:
        load.wait()
    size = len(BUFFERS)
    bufs = [dict(zip(BUFFERS, scratch[i * size : (i + 1) * size])) for i in range(SLOTS * TOGETHER)]
    lane = lax.broadcasted_iota(jnp.int32, (1, BS), 1)
    dual[...] = jnp.full(dual.shape, -1.0, jnp.float32)

    def prepare(t, b):
        s = listed[0, t]
        x = vox[pl.ds(s, 3, stride=VB), :] - 0.5
        xh = f32(bf(x))
        xl = x - xh
        tops = [f32(ypool[pidx[s * KC + k], 0:8, :]) for k in range(KC)]
        while len(tops) > 1:
            tops = [jnp.maximum(a, c) for a, c in zip(tops[::2], tops[1::2])]
        top = jnp.max(tops[0][3:4], axis=1, keepdims=True)
        top = jnp.broadcast_to(top, (1, BS))
        one = jnp.ones((1, BS), jnp.float32)
        xa = jnp.concatenate([xh, one, xh, one, xl, one, xl, -top], axis=0)
        b["xat"][...] = bf(xa.T)
        b["top"][0:1, :] = top

    def score(t, b, c):
        s = listed[0, t]
        y = [ypool[pidx[s * KC + 2 * c + j]] for j in range(2)]
        return jnp.dot(
            b["xat"][...], jnp.concatenate(y, axis=1), preferred_element_type=jnp.float32
        )

    def spread(t, b, c):
        s = listed[0, t]
        e = jnp.concatenate([b["split"][2 * c], b["split"][2 * c + 1]], axis=1)
        m = jnp.dot(b["f8"][...], e, preferred_element_type=jnp.float32)
        for j in range(2):
            mom[pidx[s * KC + 2 * c + j]] += m[:, j * BS : (j + 1) * BS]

    def weigh(sc, b, c, part):
        e = jnp.exp2(sc)
        eh = bf(e)
        el = bf(e - f32(eh))
        for j in range(2):
            b["split"][2 * c + j, 0:BS, :] = eh[:, j * BS : (j + 1) * BS]
            b["split"][2 * c + j, BS:, :] = el[:, j * BS : (j + 1) * BS]
        p = e[:, :BS] + e[:, BS:]
        return p if part is None else part + p

    def weigh_and_spread(new, old):
        parts = [None] * len(new)
        for c in range(KC // 2):
            scores = [score(t, b, c) for t, b in new]
            for t, b in old:
                spread(t, b, c)
            parts = [weigh(sc, b, c, p) for sc, (t, b), p in zip(scores, new, parts)]
        for p, (t, b) in zip(parts, new):
            b["part"][...] = p

    def norm(t, b):
        s = listed[0, t]
        d = jnp.sum(b["part"][...].T, axis=0, keepdims=True)
        xr = vox[pl.ds(s, 3, stride=VB), :]
        x = xr - 0.5
        sq = jnp.sum(x * x, axis=0, keepdims=True)
        where = listed[1, t]
        top_row = (where >> 16) * GROUP
        rank = (where >> 8) & 255
        mark = pl.ds(top_row + PAIR_CAP, 1)
        dual[mark, :] = jnp.where(
            lane == first_lane + rank, (where & 255).astype(jnp.float32), dual[mark, :]
        )
        dual[pl.ds(top_row + rank, 1), :] = (1.0 / EPS) * sq - LN2 * (b["top"][0:1, :] + jnp.log2(d))
        w = mass[pl.ds(s, 1), :] / d
        f = jnp.concatenate([w, xr * w], axis=0)
        fh = f32(bf(f))
        f8 = bf(jnp.concatenate([fh, f - fh], axis=0))
        b["f8"][...] = jnp.concatenate([f8, f8], axis=1)

    def step(g, slot, valid):
        def blocks(lag):
            if not valid(lag):
                return []
            first = ((slot - lag) % SLOTS) * TOGETHER
            return [((g - lag) * TOGETHER + u, bufs[first + u]) for u in range(TOGETHER)]

        new, old = blocks(1), blocks(3)
        for u in range(0, TOGETHER, 2):
            weigh_and_spread(new[u : u + 2], old[u : u + 2])
        for t, b in blocks(0):
            prepare(t, b)
        for t, b in blocks(2):
            norm(t, b)

    groups = n // TOGETHER

    @pl.when(n > 0)
    def _():
        for g in range(SLOTS):
            step(g, g, lambda lag: lag <= g)

        @pl.loop(0, (groups - SLOTS) // SLOTS)
        def _(h):
            for u in range(SLOTS):
                step(SLOTS + SLOTS * h + u, u, lambda lag: True)

        for e in range(3):
            step(groups + e, e, lambda lag: lag > e)

    for q, out in enumerate((low_out, own_out, high_out)):

        @pl.loop(0, SB // 16)
        def _(g):
            for j in range(16):
                m = mom[q * SB + g * 16 + j]
                out[g * 16 + j] = m[0:4] + m[4:8]


def work(pidx, listed, vox, mass, ypool):
    moments = jax.ShapeDtypeStruct((SB, 4, BS), jnp.float32)
    scratch = [
        pltpu.VMEM((POOL, 8, BS), jnp.float32),
        pltpu.VMEM((3 * VB, BS), jnp.float32),
        pltpu.VMEM((VB, BS), jnp.float32),
        pltpu.SemaphoreType.DMA((2,)),
    ]
    scratch += [
        pltpu.VMEM((KC, 2 * BS, BS), jnp.bfloat16),
        pltpu.VMEM((BS, 16), jnp.bfloat16),
        pltpu.VMEM((BS, BS), jnp.float32),
        pltpu.VMEM((8, BS), jnp.float32),
        pltpu.VMEM((8, 2 * BS), jnp.bfloat16),
    ] * (SLOTS * TOGETHER)
    return pl.pallas_call(
        work_kernel,
        in_specs=[SMEM] * 2 + [HBM] * 2 + [VMEM],
        out_specs=[VMEM] * 4,
        out_shape=[moments] * 3 + [jax.ShapeDtypeStruct((N_GY * GROUP, BS), jnp.float32)],
        scratch_shapes=scratch,
        compiler_params=pltpu.CompilerParams(vmem_limit_bytes=32 << 20),
        name="work",
    )(
        pidx,
        listed,
        pltpu.with_memory_space_constraint(vox, pltpu.HBM),
        pltpu.with_memory_space_constraint(mass, pltpu.HBM),
        ypool,
    )


def on_device(
    voxel_xyz, voxel_mass, candidates, offload_plan, seed_xyz, seed_pot, seed_target, seed_home
):
    ypool, pidx, listed = exchange(
        jnp.transpose(seed_xyz, (1, 0, 2)),
        seed_pot,
        candidates.T,
        seed_home,
        offload_plan.reshape(VB // BS, BS),
    )
    vox = jnp.transpose(voxel_xyz, (1, 0, 2)).reshape(3 * VB, BS)
    low, own, high, dual = work(pidx, listed, vox, voxel_mass, ypool)
    flat = lambda m: m.reshape(4 * SB, BS)
    above_in, below_in, placed = deliver(flat(low), flat(high), dual.reshape(N_GY, GROUP, BS))
    dual_pot, moments, new_pot = total(
        flat(own), above_in, below_in, placed, seed_pot, seed_target
    )
    return (dual_pot, moments.reshape(SB, 4, BS), new_pot)


def solution(mesh):
    return jax.shard_map(
        on_device,
        mesh=mesh,
        in_specs=(
            P(("gx", "gy"), None, None),
            P(("gx", "gy"), None),
            P(("gx", "gy"), None),
            P(("gx", "gy")),
            P(("gx", "gy"), None, None),
            P(("gx", "gy"), None),
            P(("gx", "gy"), None),
            P(),
        ),
        out_specs=(P(("gx", "gy"), None), P(("gx", "gy"), None, None), P(("gx", "gy"), None)),
        check_vma=False,
    )
```

```python
import math

import jax
import jax.numpy as jnp
from jax import lax
from jax.experimental import pallas as pl
from jax.experimental.pallas import tpu as pltpu
from jax.sharding import PartitionSpec as P

BS = 128
KC = 8
PAIR_CAP = 32
VB = 256
SB = 512
POOL = 3 * SB
N_GX = 16
N_GY = 8
ROWS = 128
GROUP = 40
SLOTS = 4
TOGETHER = 4
CHUNKS = 8

EPS = 0.05
STEP = 0.5
LOG2E = math.log2(math.e)
LN2 = math.log(2.0)

VMEM = pl.BlockSpec(memory_space=pltpu.VMEM)
SMEM = pl.BlockSpec(memory_space=pltpu.SMEM)
HBM = pl.BlockSpec(memory_space=pltpu.HBM)
MESH = pl.DeviceIdType.MESH


def bf(x):
    return x.astype(jnp.bfloat16)


def f32(x):
    return x.astype(jnp.float32)


def meet(peers):
    barrier = pltpu.get_barrier_semaphore()
    for peer in peers:
        pl.semaphore_signal(barrier, inc=1, device_id=peer, device_id_type=MESH)
    pl.semaphore_wait(barrier, len(peers))


def exchange_kernel(
    xyz_hbm, pot_hbm, cand_hbm, home_hbm, plan_hbm, ypool, pidx, listed,
    xyz, pot, plane, cand, home, plan, load_sem, send_sem, recv_sem,
):
    x, g = lax.axis_index("gx"), lax.axis_index("gy")
    below, above = (x + N_GX - 1) % N_GX, (x + 1) % N_GX
    pairs = (
        (xyz_hbm, xyz.at[1]), (pot_hbm, pot.at[1]), (cand_hbm, cand), (home_hbm, home),
        (plan_hbm, plan),
    )
    loads = [pltpu.make_async_copy(a, b, load_sem.at[i]) for i, (a, b) in enumerate(pairs)]
    for load in loads:
        load.start()
    meet([(below, g), (above, g)])
    copies = []
    for q in range(CHUNKS):
        some = pl.ds(q * (SB // CHUNKS), SB // CHUNKS)
        for way, (slot, peer) in enumerate(((0, above), (2, below))):
            for kind, (source, dest) in enumerate(
                (
                    (xyz_hbm.at[:, some, :], xyz.at[slot, :, some, :]),
                    (pot_hbm.at[some, :], pot.at[slot, some, :]),
                )
            ):
                i = (q * 2 + way) * 2 + kind
                copy = pltpu.make_async_remote_copy(
                    source, dest, send_sem.at[i], recv_sem.at[i],
                    device_id=(peer, g), device_id_type=MESH,
                )
                copy.start()
                copies.append(copy)

    sub = lax.broadcasted_iota(jnp.int32, (8, BS), 0)
    low = sub < 4

    def build(slot, start, count):
        @pl.loop(0, count // 16)
        def _(i):
            at = pl.multiple_of(start + i * 16, 16)
            square = None
            for c in range(3):
                y = xyz[slot, c, pl.ds(at, 16), :] - 0.5
                plane[c * 16 : (c + 1) * 16, :] = (2.0 * LOG2E / EPS) * y
                square = y * y if square is None else square + y * y
            plane[48:64, :] = LOG2E * (pot[slot, pl.ds(at, 16), :] - (1.0 / EPS) * square)
            for j in range(16):
                t = plane[pl.ds(j, 4, stride=16), :]
                a = jnp.concatenate([t, t], axis=0)
                hi = f32(bf(a))
                mid = f32(bf(a - hi))
                first = jnp.where(low, hi, mid)
                second = jnp.where(sub == 3, a - hi - mid, jnp.where(sub == 7, 1.0, first))
                ypool[slot * SB + at + j] = bf(jnp.concatenate([first, second], axis=0))

    loads[0].wait()
    loads[1].wait()
    build(1, 0, SB)
    loads[4].wait()
    p = jnp.concatenate([plan[0:1, :], plan[1:2, :]], axis=1)
    wide = lambda axis, rows: lax.broadcasted_iota(jnp.int32, (rows, VB), axis)
    taken = jnp.broadcast_to(p >= 0, (8, VB))
    dest = jnp.broadcast_to((p >> 7) & 7, (8, VB))
    one_hot = jnp.where(taken, jnp.where(dest == wide(0, 8), 1.0, 0.0), 0.0)
    before = jnp.where(wide(0, VB) < wide(1, VB), 1.0, 0.0)
    earlier = jnp.dot(bf(one_hot), bf(before), preferred_element_type=jnp.float32)
    rank = jnp.sum(earlier * one_hot, axis=0, keepdims=True)
    place = jnp.sum(earlier, axis=0, keepdims=True)
    place = jnp.where(p >= 0, place, -1.0)
    chosen = jnp.where(place == wide(0, VB).astype(jnp.float32), 1.0, 0.0)
    facts = [
        wide(1, 1).astype(jnp.float32),
        ((p >> 7) & 7).astype(jnp.float32),
        rank,
        (p & 127).astype(jnp.float32),
        jnp.zeros((4, VB), jnp.float32),
    ]
    facts = lax.dot_general(
        bf(jnp.concatenate(facts, axis=0)),
        bf(chosen),
        (((1,), (1,)), ((), ())),
        preferred_element_type=jnp.float32,
    ).astype(jnp.int32)
    count = jnp.sum(one_hot, axis=(0, 1), keepdims=True).astype(jnp.int32)
    listed[0:1, :] = facts[0:1]
    listed[1:2, :] = (facts[1:2] << 16) | (facts[2:3] << 8) | facts[3:4]
    listed[2:8, :] = jnp.broadcast_to(count, (6, VB))
    loads[2].wait()
    loads[3].wait()

    @pl.loop(0, VB // 2)
    def _(h):
        for u in range(2):
            v = 2 * h + u
            for k in range(KC):
                s = home[cand[k, v]]
                pidx[v * KC + k] = ((((s >> 12) - x + 1) & 15) << 9) | (s & 511)

    for q in range(CHUNKS):
        for copy in copies[4 * q : 4 * q + 4]:
            copy.wait_recv()
        for slot in (0, 2):
            build(slot, q * (SB // CHUNKS), SB // CHUNKS)
    for copy in copies:
        copy.wait_send()


def exchange(xyz, pot, cand, home, plan):
    return pl.pallas_call(
        exchange_kernel,
        in_specs=[HBM] * 5,
        out_specs=[VMEM, SMEM, VMEM],
        out_shape=[
            jax.ShapeDtypeStruct((POOL, 16, BS), jnp.bfloat16),
            jax.ShapeDtypeStruct((VB * KC,), jnp.int32),
            jax.ShapeDtypeStruct((8, VB), jnp.int32),
        ],
        scratch_shapes=[
            pltpu.VMEM((3, 3, SB, BS), jnp.float32),
            pltpu.VMEM((3, SB, BS), jnp.float32),
            pltpu.VMEM((128, BS), jnp.float32),
            pltpu.SMEM((KC, VB), jnp.int32),
            pltpu.SMEM((N_GX * N_GY * SB,), jnp.int32),
            pltpu.VMEM((VB // BS, BS), jnp.int32),
            pltpu.SemaphoreType.DMA((5,)),
            pltpu.SemaphoreType.DMA((4 * CHUNKS,)),
            pltpu.SemaphoreType.DMA((4 * CHUNKS,)),
        ],
        compiler_params=pltpu.CompilerParams(
            collective_id=0, has_side_effects=True, vmem_limit_bytes=16 << 20
        ),
        name="exchange",
    )(*(pltpu.with_memory_space_constraint(a, pltpu.HBM) for a in (xyz, pot, cand, home, plan)))


def deliver_kernel(
    low, high, dual, above_in, below_in, dual_pot,
    got, dual_send, dual_recv, send_sem, recv_sem, own_sem,
):
    x, g = lax.axis_index("gx"), lax.axis_index("gy")
    below, above = (x + N_GX - 1) % N_GX, (x + 1) % N_GX
    others = [(g + d) % N_GY for d in range(1, N_GY)]
    meet([(below, g), (above, g)] + [(x, peer) for peer in others])
    copies = [
        pltpu.make_async_remote_copy(
            low, above_in, send_sem.at[0], recv_sem.at[0],
            device_id=(below, g), device_id_type=MESH,
        ),
        pltpu.make_async_remote_copy(
            high, below_in, send_sem.at[1], recv_sem.at[1],
            device_id=(above, g), device_id_type=MESH,
        ),
    ]
    for d, peer in enumerate(others):
        copies.append(
            pltpu.make_async_remote_copy(
                dual.at[peer], got.at[g], dual_send.at[d], dual_recv.at[d],
                device_id=(x, peer), device_id_type=MESH,
            )
        )
    keep = pltpu.make_async_copy(dual.at[g], got.at[g], own_sem)
    for copy in copies:
        copy.start()
    keep.start()
    keep.wait()
    for copy in copies[2:]:
        copy.wait()
    row = lax.broadcasted_iota(jnp.int32, (ROWS, BS), 0).astype(jnp.float32)
    total = None
    for half in range(2):
        fill = None
        for j in range(4):
            index = got[4 * half + j, PAIR_CAP : PAIR_CAP + 1, :]
            fill = index if fill is None else jnp.maximum(fill, index)
        hot = bf(jnp.where(row == fill, 1.0, 0.0))
        rest = jnp.concatenate([got[4 * half + j, :PAIR_CAP, :] for j in range(4)], axis=0)
        for _ in range(3):
            piece = bf(rest)
            rest = rest - f32(piece)
            term = jnp.dot(hot, piece, preferred_element_type=jnp.float32)
            total = term if total is None else total + term
    dual_pot[...] = total
    for copy in copies[:2]:
        copy.wait()


def deliver(low, high, dual):
    moments = jax.ShapeDtypeStruct((4 * SB, BS), jnp.float32)
    return pl.pallas_call(
        deliver_kernel,
        in_specs=[VMEM] * 3,
        out_specs=[VMEM] * 3,
        out_shape=[moments] * 2 + [jax.ShapeDtypeStruct((ROWS, BS), jnp.float32)],
        scratch_shapes=[
            pltpu.VMEM((N_GY, GROUP, BS), jnp.float32),
            pltpu.SemaphoreType.DMA((N_GY - 1,)),
            pltpu.SemaphoreType.DMA((N_GY - 1,)),
            pltpu.SemaphoreType.DMA((2,)),
            pltpu.SemaphoreType.DMA((2,)),
            pltpu.SemaphoreType.DMA(()),
        ],
        compiler_params=pltpu.CompilerParams(
            collective_id=1, has_side_effects=True, vmem_limit_bytes=16 << 20
        ),
        name="deliver",
    )(low, high, dual)


def total_kernel(
    own, above_in, below_in, dual_pot, pot, target, dual_hbm, moments_hbm, new_pot_hbm,
    moments, new_pot, sems,
):
    parts = 4
    size = 4 * SB // parts
    sends = [pltpu.make_async_copy(dual_pot, dual_hbm, sems.at[parts + 1])]
    sends[0].start()
    for q in range(parts):

        @pl.loop(0, SB // 16 // parts)
        def _(i):
            at = pl.multiple_of(q * size + i * 64, 64)
            moments[pl.ds(at, 64), :] = (
                own[pl.ds(at, 64), :] + above_in[pl.ds(at, 64), :] + below_in[pl.ds(at, 64), :]
            )
            for j in range(2):
                rows = pl.ds(pl.multiple_of(q * (size // 4) + i * 16, 16) + 8 * j, 8)
                mass = moments[pl.ds(at + 32 * j, 8, stride=4), :]
                new_pot[rows, :] = pot[rows, :] + STEP * (target[rows, :] - mass)

        some = pl.ds(q * size, size)
        sends.append(pltpu.make_async_copy(moments.at[some], moments_hbm.at[some], sems.at[q]))
        sends[-1].start()
    sends.append(pltpu.make_async_copy(new_pot, new_pot_hbm, sems.at[parts]))
    sends[-1].start()
    for send in sends:
        send.wait()


def total(own, above_in, below_in, dual_pot, pot, target):
    shapes = [(ROWS, BS), (4 * SB, BS), (SB, BS)]
    return pl.pallas_call(
        total_kernel,
        in_specs=[VMEM] * 6,
        out_specs=[HBM] * 3,
        out_shape=[jax.ShapeDtypeStruct(shape, jnp.float32) for shape in shapes],
        scratch_shapes=[
            pltpu.VMEM((4 * SB, BS), jnp.float32),
            pltpu.VMEM((SB, BS), jnp.float32),
            pltpu.SemaphoreType.DMA((6,)),
        ],
        compiler_params=pltpu.CompilerParams(vmem_limit_bytes=16 << 20),
        name="total",
    )(own, above_in, below_in, dual_pot, pot, target)


BUFFERS = ("split", "xat", "part", "top", "f8")


def work_kernel(
    pidx, listed, vox_hbm, mass_hbm, ypool,
    low_out, own_out, high_out, dual, mom, vox, mass, sems, *scratch,
):
    loads = [
        pltpu.make_async_copy(vox_hbm, vox.at[pl.ds(0, 3 * VB)], sems.at[0]),
        pltpu.make_async_copy(mass_hbm, mass, sems.at[1]),
    ]
    for load in loads:
        load.start()
    first_lane = (lax.axis_index("gy") & 3) * PAIR_CAP
    n = listed[2, 0]

    @pl.loop(0, POOL // 16)
    def _(i):
        for j in range(16):
            mom[i * 16 + j] = jnp.zeros((8, BS), jnp.float32)

    for load in loads:
        load.wait()
    size = len(BUFFERS)
    bufs = [dict(zip(BUFFERS, scratch[i * size : (i + 1) * size])) for i in range(SLOTS * TOGETHER)]
    lane = lax.broadcasted_iota(jnp.int32, (1, BS), 1)
    dual[...] = jnp.full(dual.shape, -1.0, jnp.float32)

    def prepare(t, b):
        s = listed[0, t]
        x = vox[pl.ds(s, 3, stride=VB), :] - 0.5
        xh = f32(bf(x))
        xl = x - xh
        tops = [f32(ypool[pidx[s * KC + k], 0:8, :]) for k in range(KC)]
        while len(tops) > 1:
            tops = [jnp.maximum(a, c) for a, c in zip(tops[::2], tops[1::2])]
        top = jnp.max(tops[0][3:4], axis=1, keepdims=True)
        top = jnp.broadcast_to(top, (1, BS))
        one = jnp.ones((1, BS), jnp.float32)
        xa = jnp.concatenate([xh, one, xh, one, xl, one, xl, -top], axis=0)
        b["xat"][...] = bf(xa.T)
        b["top"][0:1, :] = top

    def score(t, b, c):
        s = listed[0, t]
        y = [ypool[pidx[s * KC + 2 * c + j]] for j in range(2)]
        return jnp.dot(
            b["xat"][...], jnp.concatenate(y, axis=1), preferred_element_type=jnp.float32
        )

    def spread(t, b, c):
        s = listed[0, t]
        e = jnp.concatenate([b["split"][2 * c], b["split"][2 * c + 1]], axis=1)
        m = jnp.dot(b["f8"][...], e, preferred_element_type=jnp.float32)
        for j in range(2):
            mom[pidx[s * KC + 2 * c + j]] += m[:, j * BS : (j + 1) * BS]

    def weigh(sc, b, c, part):
        e = jnp.exp2(sc)
        eh = bf(e)
        el = bf(e - f32(eh))
        for j in range(2):
            b["split"][2 * c + j, 0:BS, :] = eh[:, j * BS : (j + 1) * BS]
            b["split"][2 * c + j, BS:, :] = el[:, j * BS : (j + 1) * BS]
        p = e[:, :BS] + e[:, BS:]
        return p if part is None else part + p

    def weigh_and_spread(new, old):
        parts = [None] * len(new)
        for c in range(KC // 2):
            scores = [score(t, b, c) for t, b in new]
            for t, b in old:
                spread(t, b, c)
            parts = [weigh(sc, b, c, p) for sc, (t, b), p in zip(scores, new, parts)]
        for p, (t, b) in zip(parts, new):
            b["part"][...] = p

    def norm(t, b):
        s = listed[0, t]
        d = jnp.sum(b["part"][...].T, axis=0, keepdims=True)
        xr = vox[pl.ds(s, 3, stride=VB), :]
        x = xr - 0.5
        sq = jnp.sum(x * x, axis=0, keepdims=True)
        where = listed[1, t]
        top_row = (where >> 16) * GROUP
        rank = (where >> 8) & 255
        mark = pl.ds(top_row + PAIR_CAP, 1)
        dual[mark, :] = jnp.where(
            lane == first_lane + rank, (where & 255).astype(jnp.float32), dual[mark, :]
        )
        dual[pl.ds(top_row + rank, 1), :] = (1.0 / EPS) * sq - LN2 * (b["top"][0:1, :] + jnp.log2(d))
        w = mass[pl.ds(s, 1), :] / d
        f = jnp.concatenate([w, xr * w], axis=0)
        fh = f32(bf(f))
        f8 = bf(jnp.concatenate([fh, f - fh], axis=0))
        b["f8"][...] = jnp.concatenate([f8, f8], axis=1)

    def step(g, slot, valid):
        def blocks(lag):
            if not valid(lag):
                return []
            first = ((slot - lag) % SLOTS) * TOGETHER
            return [((g - lag) * TOGETHER + u, bufs[first + u]) for u in range(TOGETHER)]

        new, old = blocks(1), blocks(3)
        for u in range(0, TOGETHER, 2):
            weigh_and_spread(new[u : u + 2], old[u : u + 2])
        for t, b in blocks(0):
            prepare(t, b)
        for t, b in blocks(2):
            norm(t, b)

    groups = n // TOGETHER

    @pl.when(n > 0)
    def _():
        for g in range(SLOTS):
            step(g, g, lambda lag: lag <= g)

        @pl.loop(0, (groups - SLOTS) // SLOTS)
        def _(h):
            for u in range(SLOTS):
                step(SLOTS + SLOTS * h + u, u, lambda lag: True)

        for e in range(3):
            step(groups + e, e, lambda lag: lag > e)

    for q, out in enumerate((low_out, own_out, high_out)):

        @pl.loop(0, SB // 16)
        def _(g):
            for j in range(16):
                m = mom[q * SB + g * 16 + j]
                out[g * 16 + j] = m[0:4] + m[4:8]


def work(pidx, listed, vox, mass, ypool):
    moments = jax.ShapeDtypeStruct((SB, 4, BS), jnp.float32)
    scratch = [
        pltpu.VMEM((POOL, 8, BS), jnp.float32),
        pltpu.VMEM((8 * VB, BS), jnp.float32),
        pltpu.VMEM((VB, BS), jnp.float32),
        pltpu.SemaphoreType.DMA((2,)),
    ]
    scratch += [
        pltpu.VMEM((KC, 2 * BS, BS), jnp.bfloat16),
        pltpu.VMEM((BS, 16), jnp.bfloat16),
        pltpu.VMEM((BS, BS), jnp.float32),
        pltpu.VMEM((8, BS), jnp.float32),
        pltpu.VMEM((8, 2 * BS), jnp.bfloat16),
    ] * (SLOTS * TOGETHER)
    return pl.pallas_call(
        work_kernel,
        in_specs=[SMEM] * 2 + [HBM] * 2 + [VMEM],
        out_specs=[VMEM] * 4,
        out_shape=[moments] * 3 + [jax.ShapeDtypeStruct((N_GY * GROUP, BS), jnp.float32)],
        scratch_shapes=scratch,
        compiler_params=pltpu.CompilerParams(vmem_limit_bytes=32 << 20),
        name="work",
    )(
        pidx,
        listed,
        pltpu.with_memory_space_constraint(vox, pltpu.HBM),
        pltpu.with_memory_space_constraint(mass, pltpu.HBM),
        ypool,
    )


def on_device(
    voxel_xyz, voxel_mass, candidates, offload_plan, seed_xyz, seed_pot, seed_target, seed_home
):
    ypool, pidx, listed = exchange(
        jnp.transpose(seed_xyz, (1, 0, 2)),
        seed_pot,
        candidates.T,
        seed_home,
        offload_plan.reshape(VB // BS, BS),
    )
    vox = jnp.transpose(voxel_xyz, (1, 0, 2)).reshape(3 * VB, BS)
    low, own, high, dual = work(pidx, listed, vox, voxel_mass, ypool)
    flat = lambda m: m.reshape(4 * SB, BS)
    above_in, below_in, placed = deliver(flat(low), flat(high), dual.reshape(N_GY, GROUP, BS))
    dual_pot, moments, new_pot = total(
        flat(own), above_in, below_in, placed, seed_pot, seed_target
    )
    return (dual_pot, moments.reshape(SB, 4, BS), new_pot)


def solution(mesh):
    return jax.shard_map(
        on_device,
        mesh=mesh,
        in_specs=(
            P(("gx", "gy"), None, None),
            P(("gx", "gy"), None),
            P(("gx", "gy"), None),
            P(("gx", "gy")),
            P(("gx", "gy"), None, None),
            P(("gx", "gy"), None),
            P(("gx", "gy"), None),
            P(),
        ),
        out_specs=(P(("gx", "gy"), None), P(("gx", "gy"), None, None), P(("gx", "gy"), None)),
        check_vma=False,
    )
```
